32 devices in a mesh: seq: 8 (over z, y), head: 4 (over x, core).
Axes of the slice: x: 2, y: 2, z: 4, core: 2. Of those that a mesh axis runs over, the one named last changes fastest.
Arguments:
- inputs: bfloat16 [2048, 2048], P('seq'), may hold values from -6 to 6
- norm_in: float32 [2048], replicated, may hold values from 0.5 to 1.5
- w_query: bfloat16 [2048, 2048], P(None, 'head'), may hold values from -0.125 to 0.125
- w_key: bfloat16 [2048, 2048], P(None, 'head'), may hold values from -0.125 to 0.125
- w_value: bfloat16 [2048, 4096], P(None, 'head'), may hold values from -0.125 to 0.125
- w_outgate: bfloat16 [2048, 4096], P(None, 'head'), may hold values from -0.125 to 0.125
- w_decay: bfloat16 [2048, 16], P(None, 'head'), may hold values from -0.125 to 0.125
- w_write: bfloat16 [2048, 16], P(None, 'head'), may hold values from -2 to 2
- conv_query: float32 [4, 2048], P(None, 'head'), may hold values from -0.5 to 0.5
- conv_key: float32 [4, 2048], P(None, 'head'), may hold values from -0.5 to 0.5
- conv_value: float32 [4, 4096], P(None, 'head'), may hold values from -0.5 to 0.5
- decay_log: float32 [16], P('head'), may hold values from -4 to 0.5
- decay_bias: float32 [16], P('head'), may hold values from -10 to -3
- norm_out: float32 [256], replicated, may hold values from 0.5 to 1.5
- w_output: bfloat16 [4096, 2048], P('head'), may hold values from -0.125 to 0.125
- norm_ffn: float32 [2048], replicated, may hold values from 0.5 to 1.5
- w_gate: bfloat16 [2048, 5504], P(None, 'head'), may hold values from -0.125 to 0.125
- w_up: bfloat16 [2048, 5504], P(None, 'head'), may hold values from -0.125 to 0.125
- w_down: bfloat16 [5504, 2048], P('head'), may hold values from -0.15625 to 0.15625
- doc_count: int32 [8], P('seq'), may hold values from 0 to 1, as said below
- doc_start: int32 [8], P('seq'), may hold values from 0 to 255, as said below
- cotangent: bfloat16 [2048, 2048], P('seq'), may hold values from -6 to 6
Outputs:
- block_out: float32 [2048, 2048], P('seq')
- grad_inputs: float32 [2048, 2048], P('seq')
- grad_norm_in: float32 [2048], P('seq')
- grad_w_query: float32 [2048, 2048], P('seq', 'head')
- grad_w_key: float32 [2048, 2048], P('seq', 'head')
- grad_w_value: float32 [2048, 4096], P('seq', 'head')
- grad_w_outgate: float32 [2048, 4096], P('seq', 'head')
- grad_w_decay: float32 [2048, 16], P('seq', 'head')
- grad_w_write: float32 [2048, 16], P('seq', 'head')
- grad_conv_query: float32 [4, 2048], P(None, 'head')
- grad_conv_key: float32 [4, 2048], P(None, 'head')
- grad_conv_value: float32 [4, 4096], P(None, 'head')
- grad_decay_log: float32 [16], P('head')
- grad_decay_bias: float32 [16], P('head')
- grad_norm_out: float32 [256], replicated
- grad_w_output: float32 [4096, 2048], P('head', 'seq')
- grad_norm_ffn: float32 [2048], P('seq')
- grad_w_gate: float32 [2048, 5504], P('seq', 'head')
- grad_w_up: float32 [2048, 5504], P('seq', 'head')
- grad_w_down: float32 [5504, 2048], P('head', 'seq')
The draws below stay inside these ranges and needn't reach their ends.
Inputs may be any that keep to these rules, and one draw needn't show every extreme that they name: `doc_count`: at most one document starts in a shard of 256 tokens; the first shard's document starts at its first token. `doc_start`: where doc_count is 0 the entry means nothing.
All inputs are finite; a program needn't handle non-finite values.
Results may differ from the reference program's by a relative error of at most 0.0098.
Values sent between devices are 32-bit elements; how exact they have to be, the bound alone decides.
No kernel may reach another device: no remote copies, remote signals or barrier semaphores. Data moves between devices by JAX's collectives and lax.ppermute only.
A program may use at most 256 MiB of HBM per device.

```python
import jax
import jax.numpy as jnp
from jax import lax

D = 2048
H = 16
DK = 128
DV = 256
FF = 5504
BLOCK = 64
CONV = 4
DOC_MIN = 2048
DOC_MAX = 8192
TOK_DEV = 256
TOKENS = 2048


def doc_layout(key):
    shards = TOKENS // TOK_DEV
    most_docs = TOKENS // DOC_MIN + 1
    doc_lengths = jax.random.randint(jax.random.fold_in(key, 7), (most_docs,), DOC_MIN, DOC_MAX + 1, dtype=jnp.int32)
    starts_all = jnp.cumsum(doc_lengths) - doc_lengths
    shard_base = jnp.arange(shards, dtype=jnp.int32) * TOK_DEV
    inside = (starts_all[None, :] >= shard_base[:, None]) & (starts_all[None, :] < shard_base[:, None] + TOK_DEV)
    counts = jnp.sum(inside.astype(jnp.int32), axis=1)
    offsets = jnp.sum(jnp.where(inside, starts_all[None, :] - shard_base[:, None], 0), axis=1)
    filler = jnp.full((shards,), TOK_DEV - 1, jnp.int32)
    return (counts, jnp.where(counts > 0, offsets, filler))


def draw_doc_count(key, part):
    return doc_layout(key)[0]


def draw_doc_start(key, part):
    return doc_layout(key)[1]


def common_offset(key):
    raw = jax.random.normal(jax.random.fold_in(key, 11), (D,), jnp.float32)
    return jnp.clip(raw, -3.0, 3.0) * 0.3


def draw_inputs(key, part):
    offset = common_offset(key)
    noise = jnp.clip(jax.random.normal(jax.random.fold_in(key, 12), (TOKENS, D), jnp.float32), -5.0, 5.0)
    return (noise + offset[None, :]).astype(jnp.bfloat16)


def draw_w_write(key, part):
    offset = common_offset(key)
    strength = jax.random.uniform(jax.random.fold_in(key, 13), (H,), jnp.float32, 2.0, 4.5) * (1.09 ** 0.5 / 0.09)
    noise = jnp.clip(jax.random.normal(jax.random.fold_in(key, 14), (D, H), jnp.float32), -5.0, 5.0) * D ** (-0.5)
    return (noise - offset[:, None] * strength[None, :] * (1.0 / D)).astype(jnp.bfloat16)


def strengthened(result, rng, source, target, shards_of, factor):
    owner, partner = [(jnp.arange(result.shape[axis_at]) // (result.shape[axis_at] // shards_of)).reshape([-1 if axis == axis_at else 1 for axis in range(result.ndim)]) for axis_at in (source, target)]
    chosen = jax.random.permutation(rng, shards_of)[partner]
    strong = (owner == chosen) | (owner == (partner + shards_of // 2) % shards_of)
    return jnp.where(strong, factor * result, result)


def shard_levels(key, shape, cuts, least, high):
    loudness, own = 1.0, jax.random.fold_in(key, 6)
    for dim, shards_of in cuts:
        draws = jnp.exp(jax.random.uniform(jax.random.fold_in(own, dim), (shards_of,), jnp.float32, least / len(cuts), high / len(cuts)))
        loudness = loudness * jnp.repeat(draws, shape[dim] // shards_of).reshape([-1 if axis == dim else 1 for axis in range(len(shape))])
    return loudness


def bell_draw(stream_key, dims, scale, most, cuts=(), kind=jnp.bfloat16):
    values = scale * jax.random.normal(stream_key, dims, jnp.float32)
    if cuts:
        values = values * shard_levels(stream_key, dims, cuts, -0.22, 0.18)
    return jnp.clip(values, -most, most).astype(kind)


def gaussian_with(rng, shape, deviation, reach, cuts, heavy, held_as=jnp.bfloat16):
    drawn = deviation * jax.random.normal(rng, shape, jnp.float32)
    if cuts:
        drawn = drawn * shard_levels(rng, shape, cuts, -0.22, 0.18)
    return jnp.clip(strengthened(drawn, jax.random.fold_in(rng, 3), *heavy), -reach, reach).astype(held_as)


def setup_inputs(seed: int = 0) -> dict:
    seeds = jax.random.split(jax.random.key(seed), 23)
    inputs = draw_inputs(jax.random.fold_in(seeds[22], 71), 0)
    norm_in = jnp.clip(1.0 + 0.1 * jax.random.normal(seeds[1], (D,), jnp.float32), 0.5, 1.5)
    w_query = bell_draw(seeds[2], (D, H * DK), D ** -0.5, 0.125, ((1, 4),))
    w_key = bell_draw(seeds[3], (D, H * DK), D ** -0.5, 0.125, ((1, 4),))
    w_value = bell_draw(seeds[4], (D, H * DV), D ** -0.5, 0.125, ((1, 4),))
    w_outgate = bell_draw(seeds[5], (D, H * DV), D ** -0.5, 0.125, ((1, 4),))
    w_decay = bell_draw(seeds[6], (D, H), D ** -0.5, 0.125, ((1, 4),))
    w_write = draw_w_write(jax.random.fold_in(seeds[22], 71), 0)
    conv_query = jnp.clip(jax.random.uniform(seeds[8], (CONV, H * DK), jnp.float32, -0.5, 0.5) * shard_levels(seeds[8], (CONV, H * DK), ((1, 4),), -0.4, 0.0), -0.5, 0.5)
    conv_key = jnp.clip(jax.random.uniform(seeds[9], (CONV, H * DK), jnp.float32, -0.5, 0.5) * shard_levels(seeds[9], (CONV, H * DK), ((1, 4),), -0.4, 0.0), -0.5, 0.5)
    conv_value = jnp.clip(jax.random.uniform(seeds[10], (CONV, H * DV), jnp.float32, -0.5, 0.5) * shard_levels(seeds[10], (CONV, H * DV), ((1, 4),), -0.4, 0.0), -0.5, 0.5)
    decay_log = jnp.clip(-4.0 + 4.5 * jax.random.uniform(seeds[11], (H,), jnp.float32) ** shard_levels(seeds[11], (H,), ((0, 4),), -0.2, 0.2), -4.0, 0.5)
    decay_bias = jnp.clip(-10.0 + 7.0 * jax.random.uniform(seeds[12], (H,), jnp.float32) ** shard_levels(seeds[12], (H,), ((0, 4),), -0.2, 0.2), -10.0, -3.0)
    norm_out = jnp.clip(1.0 + 0.1 * jax.random.normal(seeds[13], (DV,), jnp.float32), 0.5, 1.5)
    w_output = bell_draw(seeds[14], (H * DV, D), (H * DV // 2) ** -0.5, 0.125, ((0, 4),))
    norm_ffn = jnp.clip(1.0 + 0.1 * jax.random.normal(seeds[15], (D,), jnp.float32), 0.5, 1.5)
    w_gate = bell_draw(seeds[16], (D, FF), D ** -0.5, 0.125, ((1, 4),))
    w_up = bell_draw(seeds[17], (D, FF), D ** -0.5, 0.125, ((1, 4),))
    w_down = bell_draw(seeds[18], (FF, D), (FF // 4) ** -0.5, 0.15625, ((0, 4),))
    doc_count = draw_doc_count(jax.random.fold_in(seeds[22], 71), 0)
    doc_start = draw_doc_start(jax.random.fold_in(seeds[22], 71), 0)
    cotangent = gaussian_with(seeds[21], (TOKENS, D), 1.0, 6.0, ((0, 8),), (0, 1, 8, 2.0))
    return dict(inputs=inputs, norm_in=norm_in, w_query=w_query, w_key=w_key, w_value=w_value, w_outgate=w_outgate, w_decay=w_decay, w_write=w_write, conv_query=conv_query, conv_key=conv_key, conv_value=conv_value, decay_log=decay_log, decay_bias=decay_bias, norm_out=norm_out, w_output=w_output, norm_ffn=norm_ffn, w_gate=w_gate, w_up=w_up, w_down=w_down, doc_count=doc_count, doc_start=doc_start, cotangent=cotangent)


PRECISE = lax.Precision.HIGHEST

@jax.custom_vjp
def low(v):
    return lax.optimization_barrier(v.astype(jnp.bfloat16)).astype(jnp.float32)

@jax.custom_vjp
def low_back(v):
    return v

def low_keep(v):
    return (low(v), None)

def low_pass(kept, grad):
    return (grad,)

def back_keep(v):
    return (v, None)

def back_low(kept, grad):
    return (low(grad),)
low.defvjp(low_keep, low_pass)
low_back.defvjp(back_keep, back_low)

def rms_scale(values, gain):
    return values * lax.rsqrt(lax.optimization_barrier(jnp.mean(values * values, axis=-1, keepdims=True)) + 1e-05) * gain

def unit_rows(values):
    return values * lax.rsqrt(lax.optimization_barrier(jnp.sum(values * values, axis=-1, keepdims=True)) + 1e-06)

def causal_conv(extended, weight, segment_wide, length):
    taps = weight.shape[0]
    summed = jnp.zeros((length, weight.shape[1]), jnp.float32)
    for tap_index in range(taps):
        source = lax.slice_in_dim(extended, tap_index, tap_index + length, axis=0)
        agree = (lax.slice_in_dim(segment_wide, tap_index, tap_index + length, axis=0) == lax.slice_in_dim(segment_wide, taps - 1, taps - 1 + length, axis=0)).astype(jnp.float32)
        summed = summed + source * weight[tap_index] * agree[:, None]
    return summed

def prepare(proj_q, proj_k, proj_v, proj_a, proj_b, halo_q, halo_k, halo_v, conv_query, conv_key, conv_value, decay_log, decay_bias, segment_wide):
    length, head_count = proj_a.shape
    key_size = proj_q.shape[1] // head_count
    value_size = proj_v.shape[1] // head_count
    queries = jax.nn.silu(causal_conv(jnp.concatenate([halo_q, proj_q], axis=0), conv_query, segment_wide, length))
    key_rows = jax.nn.silu(causal_conv(jnp.concatenate([halo_k, proj_k], axis=0), conv_key, segment_wide, length))
    value_rows = jax.nn.silu(causal_conv(jnp.concatenate([halo_v, proj_v], axis=0), conv_value, segment_wide, length))
    queries = unit_rows(queries.reshape(length, head_count, key_size)) * key_size ** (-0.5)
    key_rows = unit_rows(key_rows.reshape(length, head_count, key_size))
    value_rows = value_rows.reshape(length, head_count, value_size)
    decays = -jnp.exp(decay_log) * jax.nn.softplus(proj_a + decay_bias)
    write_rate = jax.nn.sigmoid(proj_b)
    return (queries, key_rows, value_rows, decays, write_rate)

def block_step(carry_in, piece):
    states, prior_segment = carry_in
    queries, key_rows, value_rows, decays, write_rate, segment = piece
    block_len = segment.shape[0]
    row_index = lax.broadcasted_iota(jnp.int32, (block_len, block_len), 0)
    column_index = lax.broadcasted_iota(jnp.int32, (block_len, block_len), 1)
    same_doc = segment[:, None] == segment[None, :]
    inclusive = (row_index >= column_index) & same_doc
    strictly = (row_index > column_index) & same_doc
    running = jnp.cumsum(decays, axis=0).T
    spread = running[:, :, None] - running[:, None, :]
    spread = jnp.where(inclusive[None], spread, 0.0)
    factors = jnp.exp(spread)
    within = jnp.where(inclusive[None], factors, 0.0)
    below = jnp.where(strictly[None], factors, 0.0)
    key_key = jnp.einsum('chk,shk->hcs', key_rows, key_rows, precision=PRECISE)
    query_key = jnp.einsum('chk,shk->hcs', queries, key_rows, precision=PRECISE)
    rates = write_rate.T
    system = jnp.eye(block_len, dtype=jnp.float32)[None] + rates[:, :, None] * below * key_key
    carried = jnp.exp(running) * (segment == prior_segment).astype(jnp.float32)[None, :]
    key_state = jnp.einsum('chk,hrk->hcr', key_rows, states, precision=PRECISE)
    targets = rates[:, :, None] * (jnp.transpose(value_rows, (1, 0, 2)) - carried[:, :, None] * key_state)
    updates = lax.linalg.triangular_solve(system, targets, left_side=True, lower=True, unit_diagonal=True)
    query_state = jnp.einsum('chk,hrk->hcr', queries, states, precision=PRECISE)
    outputs = carried[:, :, None] * query_state + jnp.einsum('hcs,hsr->hcr', within * query_key, updates, precision=PRECISE)
    final_segment = segment[block_len - 1]
    ending = jnp.exp(running[:, block_len - 1:] - running) * (segment == final_segment).astype(jnp.float32)[None, :]
    keeping = jnp.exp(running[:, block_len - 1]) * (final_segment == prior_segment).astype(jnp.float32)
    fresh = keeping[:, None, None] * states + jnp.einsum('hcr,chk->hrk', updates * ending[:, :, None], key_rows, precision=PRECISE)
    return ((fresh, final_segment), jnp.transpose(outputs, (1, 0, 2)))

def delta_run(states, queries, key_rows, value_rows, decays, write_rate, segment, first_segment, block_size):
    length = key_rows.shape[0]
    blocks = length // block_size

    def by_blocks(tensor):
        return tensor.reshape((blocks, block_size) + tensor.shape[1:])
    pieces = (by_blocks(queries), by_blocks(key_rows), by_blocks(value_rows), by_blocks(decays), by_blocks(write_rate), by_blocks(segment))
    final_carry, outputs = lax.scan(jax.checkpoint(block_step), (states, first_segment), pieces)
    return (outputs.reshape((length,) + outputs.shape[2:]), final_carry[0])

def gated_norm(mixed_out, outgate, gain):
    length, head_count, value_size = mixed_out.shape
    scaled = rms_scale(mixed_out, gain)
    return (scaled * jax.nn.silu(outgate.reshape(length, head_count, value_size))).reshape(length, head_count * value_size)

def forward(inputs, norm_in, w_query, w_key, w_value, w_outgate, w_decay, w_write, conv_query, conv_key, conv_value, decay_log, decay_bias, norm_out, w_output, norm_ffn, w_gate, w_up, w_down, segment):
    normed = low(rms_scale(inputs, norm_in))
    proj_q = low_back(jnp.dot(normed, w_query, precision=PRECISE))
    proj_k = low_back(jnp.dot(normed, w_key, precision=PRECISE))
    proj_v = low_back(jnp.dot(normed, w_value, precision=PRECISE))
    proj_z = low_back(jnp.dot(normed, w_outgate, precision=PRECISE))
    proj_a = low_back(jnp.dot(normed, w_decay, precision=PRECISE))
    proj_b = low_back(jnp.dot(normed, w_write, precision=PRECISE))
    rim_rows = conv_query.shape[0] - 1
    segment_wide = jnp.concatenate([jnp.full((rim_rows,), -1.0, jnp.float32), segment])
    halo_q = jnp.zeros((rim_rows, proj_q.shape[1]), jnp.float32)
    halo_k = jnp.zeros((rim_rows, proj_k.shape[1]), jnp.float32)
    halo_v = jnp.zeros((rim_rows, proj_v.shape[1]), jnp.float32)
    queries, key_rows, value_rows, decays, write_rate = prepare(proj_q, proj_k, proj_v, proj_a, proj_b, halo_q, halo_k, halo_v, conv_query, conv_key, conv_value, decay_log, decay_bias, segment_wide)
    head_count = decay_log.shape[0]
    zero_states = jnp.zeros((head_count, value_rows.shape[2], key_rows.shape[2]), jnp.float32)
    mixed_out, _ = delta_run(zero_states, queries, key_rows, value_rows, decays, write_rate, segment, jnp.full((), -1.0, jnp.float32), BLOCK)
    gated = low(gated_norm(mixed_out, proj_z, norm_out))
    branch = low_back(jnp.dot(gated, w_output, precision=PRECISE))
    middle = inputs + branch
    normed_ffn = low(rms_scale(middle, norm_ffn))
    gate_pre = low_back(jnp.dot(normed_ffn, w_gate, precision=PRECISE))
    up_pre = low_back(jnp.dot(normed_ffn, w_up, precision=PRECISE))
    hidden = low(jax.nn.silu(gate_pre) * up_pre)
    ffn_out = low_back(jnp.dot(hidden, w_down, precision=PRECISE))
    return middle + ffn_out

def reference(inputs, norm_in, w_query, w_key, w_value, w_outgate, w_decay, w_write, conv_query, conv_key, conv_value, decay_log, decay_bias, norm_out, w_output, norm_ffn, w_gate, w_up, w_down, doc_count, doc_start, cotangent):
    length = inputs.shape[0]
    positions = jnp.arange(length, dtype=jnp.int32)
    shard_of = positions // TOK_DEV
    within_shard = positions % TOK_DEV
    has_start = (doc_count > 0).astype(jnp.int32)
    starts_before = jnp.cumsum(has_start) - has_start
    after_start = ((has_start[shard_of] > 0) & (within_shard >= doc_start[shard_of])).astype(jnp.int32)
    segment = (starts_before[shard_of] + after_start).astype(jnp.float32)
    params = (inputs.astype(jnp.float32), norm_in, w_query.astype(jnp.float32), w_key.astype(jnp.float32), w_value.astype(jnp.float32), w_outgate.astype(jnp.float32), w_decay.astype(jnp.float32), w_write.astype(jnp.float32), conv_query, conv_key, conv_value, decay_log, decay_bias, norm_out, w_output.astype(jnp.float32), norm_ffn, w_gate.astype(jnp.float32), w_up.astype(jnp.float32), w_down.astype(jnp.float32))

    def whole(*operands):
        return forward(*operands, segment)
    block_out, back = jax.vjp(whole, *params)
    grads = back(cotangent.astype(jnp.float32))
    return (block_out, grads[0], grads[1], grads[2], grads[3], grads[4], grads[5], grads[6], grads[7], grads[8], grads[9], grads[10], grads[11], grads[12], grads[13], grads[14], grads[15], grads[16], grads[17], grads[18])
```

```python
import functools
import jax
import jax.numpy as jnp
from jax import lax
from jax.experimental import pallas as pl
from jax.experimental.pallas import tpu as pltpu
from jax.sharding import PartitionSpec as P

F32 = jnp.float32
BF16 = jnp.bfloat16
HALO = 8
VMEM_LIMIT = 56 * 1024 * 1024


def split_low(a):
    high = a.astype(BF16)
    return high, (a - high.astype(F32)).astype(BF16)


def dot_low(a, b, ca, cb):
    return lax.dot_general(
        a.astype(BF16), b.astype(BF16), (((ca,), (cb,)), ((), ())), preferred_element_type=F32
    )


def dot_fine(a, b, ca, cb):
    ah, al = split_low(a)
    bh, bl = split_low(b)
    dims = (((ca,), (cb,)), ((), ()))
    one = functools.partial(lax.dot_general, dimension_numbers=dims, preferred_element_type=F32)
    return one(ah, bh) + (one(ah, bl) + one(al, bh))


def grid_iota(size):
    return (
        lax.broadcasted_iota(jnp.int32, (size, size), 0),
        lax.broadcasted_iota(jnp.int32, (size, size), 1),
    )


def lane_pick(x, index):
    lanes = lax.broadcasted_iota(jnp.int32, x.shape, 1)
    return jnp.sum(jnp.where(lanes == index, x, 0.0), axis=1, keepdims=True)


def to_row(column, eye):
    return jnp.sum(jnp.where(eye, column, 0.0), axis=0, keepdims=True)


def agree_mask(length, steps, start):
    at = lax.broadcasted_iota(jnp.int32, (length, 1), 0)
    return ((at >= start) == (at - steps >= start)).astype(F32)


def conv_forward(extended, weight, start):
    length, taps = extended.shape[0] - HALO, weight.shape[0]
    total = None
    for steps in range(taps):
        moved = extended if steps == 0 else pltpu.roll(extended, steps, 0)
        term = moved[HALO:] * weight[taps - 1 - steps : taps - steps] * agree_mask(length, steps, start)
        total = term if total is None else total + term
    return total


def conv_backward(grad, extended, weight, start):
    rows, taps = extended.shape[0], weight.shape[0]
    length = rows - HALO
    total, per_tap = None, [None] * taps
    for steps in range(taps):
        masked = grad * agree_mask(length, steps, start)
        moved = extended if steps == 0 else pltpu.roll(extended, steps, 0)
        per_tap[taps - 1 - steps] = jnp.sum(masked * moved[HALO:], axis=0, keepdims=True)
        term = jnp.concatenate([jnp.zeros((HALO, grad.shape[1]), F32), masked], axis=0)
        term = term * weight[taps - 1 - steps : taps - steps]
        term = term if steps == 0 else pltpu.roll(term, rows - steps, 0)
        total = term if total is None else total + term
    return total, jnp.concatenate(per_tap, axis=0)


def unit_forward(values):
    return values * lax.rsqrt(jnp.sum(values * values, axis=-1, keepdims=True) + 1e-06)


def unit_backward(grad, values):
    scale = lax.rsqrt(jnp.sum(values * values, axis=-1, keepdims=True) + 1e-06)
    unit = values * scale
    return scale * (grad - unit * jnp.sum(unit * grad, axis=-1, keepdims=True))


def silu_slope(pre):
    gate = jax.nn.sigmoid(pre)
    return gate * (1.0 + pre * (1.0 - gate))


def head_terms(step_log, start, length):
    rows, cols = grid_iota(length)
    eye = rows == cols
    running = jnp.sum(jnp.where(rows >= cols, to_row(step_log, eye), 0.0), axis=1, keepdims=True)
    running_row = to_row(running, eye)
    same = (rows >= start) == (cols >= start)
    inclusive = (rows >= cols) & same
    within = jnp.where(inclusive, jnp.exp(jnp.where(inclusive, running - running_row, 0.0)), 0.0)
    below = jnp.where(rows > cols, within, 0.0)
    at = lax.broadcasted_iota(jnp.int32, (length, 1), 0)
    carried = jnp.exp(running) * (at < start).astype(F32)
    total = jnp.sum(step_log, axis=0, keepdims=True)
    last_old = length - 1 < start
    ending = jnp.exp(total - running) * ((at < start) == last_old).astype(F32)
    keeping = jnp.exp(total) * jnp.where(last_old, 1.0, 0.0)
    return within, below, carried, ending, keeping


def tri_inverse(lower, length):
    rows, cols = grid_iota(length)
    near = (rows >> 1) == (cols >> 1)
    start = jnp.where(rows == cols, 1.0, 0.0) - jnp.where(near, lower, 0.0)

    def merge(level, inverse):
        apart = lax.shift_right_logical(rows, level) != lax.shift_right_logical(cols, level)
        joined = lax.shift_right_logical(rows, level + 1) == lax.shift_right_logical(cols, level + 1)
        off = jnp.where(apart & joined, lower, 0.0)
        return inverse - dot_fine(inverse, dot_fine(off, inverse, 1, 0), 1, 0)

    return lax.fori_loop(1, length.bit_length() - 1, merge, start)


def prepared(q_ref, k_ref, v_ref, hq_ref, hk_ref, hv_ref, cq_ref, ck_ref, cv_ref, start):
    ext_q = jnp.concatenate([hq_ref[...], q_ref[...]], axis=0)
    ext_k = jnp.concatenate([hk_ref[...], k_ref[...]], axis=0)
    ext_v = jnp.concatenate([hv_ref[...], v_ref[...]], axis=0)
    pre_q = conv_forward(ext_q, cq_ref[...], start)
    pre_k = conv_forward(ext_k, ck_ref[...], start)
    pre_v = conv_forward(ext_v, cv_ref[...], start)
    return (ext_q, ext_k, ext_v), (pre_q, pre_k, pre_v)


def local_kernel(
    heads, group, rows_per,
    place_ref, q_ref, k_ref, v_ref, hq_ref, hk_ref, hv_ref, cq_ref, ck_ref, cv_ref, gates_ref,
    inverse_ref, fresh_ref, erase_ref, mixed_ref, reach_ref, pack_ref,
):
    head = pl.program_id(0)
    start, me = place_ref[0], place_ref[1]
    length, key_size = q_ref.shape
    _, (pre_q, pre_k, pre_v) = prepared(
        q_ref, k_ref, v_ref, hq_ref, hk_ref, hv_ref, cq_ref, ck_ref, cv_ref, start
    )
    queries = unit_forward(jax.nn.silu(pre_q)) * key_size ** (-0.5)
    keys = unit_forward(jax.nn.silu(pre_k))
    values = jax.nn.silu(pre_v)
    step_log = lane_pick(gates_ref[...], head)
    rate = lane_pick(gates_ref[...], head + heads)
    within, below, carried, ending, keeping = head_terms(step_log, start, length)
    inverse = tri_inverse(rate * below * dot_fine(keys, keys, 1, 1), length)
    fresh = dot_fine(inverse, rate * values, 1, 0)
    erase = dot_fine(inverse, rate * carried * keys, 1, 0)
    attend = within * dot_fine(queries, keys, 1, 1)
    inverse_ref[...] = inverse
    fresh_ref[...] = fresh
    erase_ref[...] = erase
    mixed_ref[...] = dot_fine(attend, fresh, 1, 0)
    reach_ref[...] = carried * queries - dot_fine(attend, erase, 1, 0)
    ended = ending * keys
    r, c = grid_iota(key_size)
    moved = jnp.where(r == c, keeping, 0.0) - dot_fine(erase, ended, 0, 0)
    added = dot_fine(fresh, ended, 0, 0)
    for g in range(group):
        slot = g ^ (me & (group - 1))
        pack_ref[slot, :key_size] = moved
        pack_ref[slot, key_size:] = added[g * rows_per : (g + 1) * rows_per]


def scan_kernel(count, rows_per, key_size, reverse, place_ref, *refs):
    me = place_ref[1]
    packs, out_ref, held = refs[:count], refs[count], refs[count + 1]
    for k in range(count):
        held[k] = packs[k][...]

    def lap(i, state):
        shard = count - 1 - i if reverse else i
        slot = shard ^ me
        out_ref[slot] = state
        moved = held[slot, :key_size]
        return dot_fine(state, moved, 1, 1 if reverse else 0) + held[slot, key_size:]

    lax.fori_loop(0, count, lap, jnp.zeros((rows_per, key_size), F32))


def gathered_state(parts, held, group, head, me, count):
    @pl.when(head == 0)
    def _():
        for k in range(count):
            held[k] = parts[k][...]

    return jnp.concatenate([held[(head * group + g) ^ me] for g in range(group)], axis=0)


def mix_kernel(count, group, place_ref, mixed_ref, reach_ref, z_ref, gain_ref, *refs):
    parts = refs[:count]
    out_ref, gated_ref, state_ref, held = refs[count:]
    head, me = pl.program_id(0), place_ref[1]
    state = gathered_state(parts, held, group, head, me, count)
    mixed = mixed_ref[...] + dot_fine(reach_ref[...], state, 1, 1)
    state_ref[...] = state
    out_ref[...] = mixed
    scaled = mixed * lax.rsqrt(jnp.mean(mixed * mixed, axis=-1, keepdims=True) + 1e-05) * gain_ref[...]
    gated_ref[...] = (scaled * jax.nn.silu(z_ref[...])).astype(gated_ref.dtype)


def gate_back_kernel(
    group, rows_per, place_ref, grad_ref, mixed_ref, z_ref, gain_ref, reach_ref,
    grad_mixed_ref, grad_z_ref, grad_gain_ref, pack_ref, share_ref,
):
    head, me = pl.program_id(0), place_ref[1]
    mixed, z, grad, gain = mixed_ref[...], z_ref[...], grad_ref[...], gain_ref[...]
    scale = lax.rsqrt(jnp.mean(mixed * mixed, axis=-1, keepdims=True) + 1e-05)
    unit = mixed * scale
    gate = jax.nn.silu(z)
    part = jnp.sum(grad * gate * unit, axis=0, keepdims=True)

    @pl.when(head == 0)
    def _():
        grad_gain_ref[...] = part

    @pl.when(head > 0)
    def _():
        grad_gain_ref[...] += part

    grad_z = grad * gain * unit * silu_slope(z)
    grad_z_ref[...] = grad_z
    width = share_ref.shape[2]
    for g in range(group):
        share_ref[g ^ (me & (group - 1))] = grad_z[:, g * width : (g + 1) * width]
    inner = grad * gate * gain
    grad_mixed = scale * (inner - unit * jnp.mean(inner * unit, axis=-1, keepdims=True))
    grad_mixed_ref[...] = grad_mixed
    back = dot_fine(grad_mixed, reach_ref[...], 0, 0)
    for g in range(group):
        pack_ref[g ^ (me & (group - 1))] = back[g * rows_per : (g + 1) * rows_per]


def back_kernel(
    heads, group, count,
    place_ref, q_ref, k_ref, v_ref, hq_ref, hk_ref, hv_ref, cq_ref, ck_ref, cv_ref, gates_ref,
    inverse_ref, fresh_ref, erase_ref, grad_ref, state_ref, *refs,
):
    parts = refs[:count]
    (gq_ref, gk_ref, gv_ref, gates_grad_ref, rim_q_ref, rim_k_ref, rim_v_ref,
     gcq_ref, gck_ref, gcv_ref, share_ref, held) = refs[count:]
    head = pl.program_id(0)
    start, me = place_ref[0], place_ref[1]
    length, key_size = q_ref.shape
    exts, (pre_q, pre_k, pre_v) = prepared(
        q_ref, k_ref, v_ref, hq_ref, hk_ref, hv_ref, cq_ref, ck_ref, cv_ref, start
    )
    act_q, act_k, values = jax.nn.silu(pre_q), jax.nn.silu(pre_k), jax.nn.silu(pre_v)
    key_scale = key_size ** (-0.5)
    queries = unit_forward(act_q) * key_scale
    keys = unit_forward(act_k)
    step_log = lane_pick(gates_ref[...], head)
    rate = lane_pick(gates_ref[...], head + heads)
    within, below, carried, ending, keeping = head_terms(step_log, start, length)
    key_key = dot_fine(keys, keys, 1, 1)
    query_key = dot_fine(queries, keys, 1, 1)
    state, grad_mixed, inverse = state_ref[...], grad_ref[...], inverse_ref[...]
    leaving = gathered_state(parts, held, group, head, me, count)
    key_state = dot_fine(keys, state, 1, 1)
    query_state = dot_fine(queries, state, 1, 1)
    updates = fresh_ref[...] - dot_fine(erase_ref[...], state, 1, 1)
    attend = within * query_key
    ended = ending * keys
    end_pull = dot_fine(keys, leaving, 1, 1)
    grad_updates = dot_fine(attend, grad_mixed, 0, 0) + ending * end_pull
    grad_targets = dot_fine(inverse, grad_updates, 0, 0)
    grad_attend = dot_fine(grad_mixed, updates, 1, 1)
    grad_system = -dot_fine(grad_targets, updates, 1, 1)
    held_values = values - carried * key_state
    grad_queries = carried * dot_fine(grad_mixed, state, 1, 0)
    grad_rate = jnp.sum(grad_targets * held_values, axis=1, keepdims=True)
    grad_values = rate * grad_targets
    pull = -(carried * grad_values)
    grad_keys = dot_fine(pull, state, 1, 0) + ending * dot_fine(updates, leaving, 1, 0)
    grad_carried = jnp.sum(grad_mixed * query_state - grad_values * key_state, axis=1, keepdims=True)
    grad_ending = jnp.sum(updates * end_pull, axis=1, keepdims=True)
    grad_keeping = jnp.sum(jnp.sum(state * leaving, axis=1, keepdims=True), axis=0, keepdims=True)
    base = grad_system * below
    grad_rate = grad_rate + jnp.sum(base * key_key, axis=1, keepdims=True)
    base = rate * base
    grad_keys = grad_keys + dot_fine(base, keys, 1, 0) + dot_fine(base, keys, 0, 0)
    pairs = grad_attend * within
    grad_queries = grad_queries + dot_fine(pairs, keys, 1, 0)
    grad_keys = grad_keys + dot_fine(pairs, queries, 0, 0)
    rows, cols = grid_iota(length)
    eye = rows == cols
    powers = jnp.where(rows > cols, base * key_key + pairs * query_key, 0.0)
    column_sum = jnp.sum(powers, axis=0, keepdims=True)
    from_columns = jnp.sum(jnp.where(eye, column_sum, 0.0), axis=1, keepdims=True)
    end_part = grad_ending * ending
    grad_running = jnp.sum(powers, axis=1, keepdims=True) - from_columns + grad_carried * carried - end_part
    whole = jnp.sum(end_part, axis=0, keepdims=True) + grad_keeping * keeping
    running_row = to_row(grad_running, eye)
    grad_step = jnp.sum(jnp.where(cols >= rows, running_row, 0.0), axis=1, keepdims=True) + whole

    lanes = lax.broadcasted_iota(jnp.int32, gates_grad_ref.shape, 1)
    mine = jnp.where(lanes == head, grad_step, 0.0) + jnp.where(lanes == head + heads, grad_rate, 0.0)

    @pl.when(head == 0)
    def _():
        gates_grad_ref[...] = mine

    @pl.when(head > 0)
    def _():
        gates_grad_ref[...] += mine

    grad_pre_q = unit_backward(grad_queries * key_scale, act_q) * silu_slope(pre_q)
    grad_pre_k = unit_backward(grad_keys, act_k) * silu_slope(pre_k)
    grad_pre_v = grad_values * silu_slope(pre_v)
    first = 0
    for grad_pre, ext, weight_ref, out_ref, rim_ref, tap_ref in (
        (grad_pre_q, exts[0], cq_ref, gq_ref, rim_q_ref, gcq_ref),
        (grad_pre_k, exts[1], ck_ref, gk_ref, rim_k_ref, gck_ref),
        (grad_pre_v, exts[2], cv_ref, gv_ref, rim_v_ref, gcv_ref),
    ):
        moved, taps = conv_backward(grad_pre, ext, weight_ref[...], start)
        out_ref[...] = moved[HALO:]
        rim_ref[...] = moved[:HALO]
        tap_ref[...] = taps
        width = grad_pre.shape[1] // group
        for g in range(group):
            slot, piece = g ^ (me & (group - 1)), moved[:, g * width : (g + 1) * width]
            share_ref[slot, :length, first : first + width] = piece[HALO:]
            share_ref[slot, length:, first : first + width] = piece[:HALO]
        first += width


def outer_kernel(count, order, gates, place_ref, *refs):
    pieces, packs = refs[:count], refs[count : 2 * count]
    gate_refs, rest = refs[2 * count : 2 * count + gates], refs[2 * count + gates :]
    (out_ref, gate_out_ref, held, rims) = rest if gates else (rest[0], None, *rest[1:])
    seams = gates > 0
    tile, me, rank = pl.program_id(0), place_ref[1], place_ref[2]
    length = pieces[0].shape[0]

    @pl.when(tile == 0)
    def _():
        if seams:
            for k in range(count):
                rims[k] = packs[k][length:]
        for t, k in enumerate(order):
            value = packs[k][:length]
            if seams:
                after = (me ^ k) + 1
                rim = rims[(after & (count - 1)) ^ me]
                rim = jnp.where(after < count, rim, 0.0)
                value = jnp.concatenate([value[: length - HALO], value[length - HALO :] + rim], axis=0)
            held[t] = value.astype(BF16)
        out_ref[...] = jnp.zeros_like(out_ref)
        if gates:
            gate_out_ref[...] = jnp.zeros_like(gate_out_ref)

    share = held[tile]
    if gates:
        every = jnp.concatenate([ref[...] for ref in gate_refs], axis=0)
        size = every.shape[0] // count
        share_gates = jnp.zeros((size, length), F32)
        for t in range(count):
            share_gates = share_gates + jnp.where(tile == t, every[t * size : (t + 1) * size], 0.0)
    for r in range(count // 2):
        for half in range(2):
            slot = (((rank ^ r) << 1) | half) ^ me
            piece = pieces[2 * r + half][...].astype(BF16)
            out_ref[slot] += dot_low(piece, share, 0, 0)
            if gates:

                @pl.when(slot == 0)
                def _(piece=piece):
                    gate_out_ref[...] += dot_low(piece, share_gates, 0, 1)


def assemble_kernel(count, widths, place_ref, *refs):
    me, held = place_ref[1], refs[-1]
    for k in range(count):
        held[k] = refs[k][...]
    for d in range(count):
        first, source = 0, held[d ^ me]
        for out_ref, width in zip(refs[count:-1], widths):
            out_ref[:, d * width : (d + 1) * width] = source[:, first : first + width]
            first += width


def ffn_kernel(count, place_ref, *refs):
    ffn_refs, cot_refs = refs[:count], refs[count : 2 * count]
    gate_w, up_w, down_w, grad_gate_ref, grad_up_ref, grad_down_ref, ffn, cot = refs[2 * count :]
    me, rank = place_ref[1], place_ref[2]
    width = ffn_refs[0].shape[1]
    for r in range(count // 2):
        for half in range(2):
            at = pl.ds(pl.multiple_of((((rank ^ r) << 1) | half) * width, width), width)
            ffn[:, at] = ffn_refs[2 * r + half][...].astype(BF16)
            cot[:, at] = cot_refs[2 * r + half][...].astype(BF16)
    gate_pre = dot_low(ffn[...], gate_w[...], 1, 0)
    up_pre = dot_low(ffn[...], up_w[...], 1, 0)
    grad_hidden = dot_low(cot[...], down_w[...], 1, 1)
    gate = jax.nn.sigmoid(gate_pre)
    active = gate_pre * gate
    hidden = (active * up_pre).astype(BF16)
    grad_up = (grad_hidden * active).astype(BF16)
    slope = gate * (1.0 + gate_pre * (1.0 - gate))
    grad_gate = (grad_hidden * up_pre * slope).astype(BF16)
    mine = pl.ds(pl.multiple_of(me * width, width), width)
    ffn_mine, cot_mine = ffn[:, mine], cot[:, mine]

    @pl.when(pl.program_id(0) == 0)
    def _():
        grad_gate_ref[...] = jnp.zeros_like(grad_gate_ref)
        grad_up_ref[...] = jnp.zeros_like(grad_up_ref)
        grad_down_ref[...] = jnp.zeros_like(grad_down_ref)

    grad_gate_ref[...] += dot_low(ffn_mine, grad_gate, 0, 0)
    grad_up_ref[...] += dot_low(ffn_mine, grad_up, 0, 0)
    grad_down_ref[...] += dot_low(hidden, cot_mine, 0, 0)


def xor_pairs(size, bit):
    return [(at, at ^ bit) for at in range(size)]


def swap(value, axis, bit):
    return lax.ppermute(value, axis, xor_pairs(lax.axis_size(axis), bit))


def shifted(value, axis, steps):
    count = lax.axis_size(axis)
    first, last = (max(0, -steps), min(count, count - steps))
    return lax.ppermute(value, axis, [(source, source + steps) for source in range(first, last)])


def exchange(parts, axis):
    return [part if k == 0 else swap(part, axis, k) for k, part in enumerate(parts)]


def head_sum(part):
    count, half = lax.axis_size("head"), part.shape[0] // 2
    mine = lax.axis_index("head") & 1
    kept = lax.dynamic_slice_in_dim(part, mine * half, half, 0)
    kept = kept + swap(lax.dynamic_slice_in_dim(part, (1 - mine) * half, half, 0), "head", 1)
    bit = 2
    while bit < count:
        kept = kept + swap(kept, "head", bit)
        bit *= 2
    other = swap(kept, "head", 1)
    low = mine == 0
    return jnp.concatenate([jnp.where(low, kept, other), jnp.where(low, other, kept)], axis=0)


def seq_sum(value):
    bit = 1
    while bit < lax.axis_size("seq"):
        value = value + swap(value, "seq", bit)
        bit *= 2
    return value


def head_total(value):
    bit = 1
    while bit < lax.axis_size("head"):
        value = value + swap(value, "head", bit)
        bit *= 2
    return value


TOKEN_ORDER = (0, 4, 2, 6, 1, 5, 3, 7)


def spread(value, steps=("far", "near", "y", "x", "c")):
    width = value.shape[1] // 4
    start = lax.axis_index("head") * width
    halves = []
    for half in range(2):
        first = lax.dynamic_slice_in_dim(value, start + half * (width // 2), width // 2, 1)
        have = {0: first}
        for step in steps:
            if step in ("x", "c"):
                bit = 2 if step == "x" else 1
                have.update({r ^ bit: swap(part, "head", bit) for r, part in have.items()})
            else:
                bit = {"far": 4, "near": 2, "y": 1}[step]
                have = {
                    r: jnp.concatenate([part, swap(part, "seq", bit)], axis=0) for r, part in have.items()
                }
        halves.append(have)
    return [halves[half][r] for r in range(4) for half in range(2)]


def rms_scale(values, gain):
    return values * lax.rsqrt(jnp.mean(values * values, axis=-1, keepdims=True) + 1e-05) * gain


def swiglu(gate_pre, up_pre):
    return jax.nn.silu(gate_pre) * up_pre


def gate_values(proj_ab, decay_log, decay_bias):
    heads = decay_log.shape[0]
    decays = -jnp.exp(decay_log) * jax.nn.softplus(proj_ab[:, :heads] + decay_bias)
    return jnp.concatenate([decays, jax.nn.sigmoid(proj_ab[:, heads:])], axis=1)


def block(shape, index):
    return pl.BlockSpec(shape, index)


class Delta:
    def __init__(self, length, heads, key_size, value_size, taps, count):
        self.length, self.heads, self.count = length, heads, count
        self.key_size, self.value_size, self.taps = key_size, value_size, taps
        self.group = count // heads
        self.rows_per = heads * value_size // count
        assert self.group * heads == count and self.group & (self.group - 1) == 0

    def cols(self, width, first=0):
        return block((self.length, width), lambda h, p: (0, h + first))

    def rim(self, width, first=0, rows=HALO):
        return block((rows, width), lambda h, p: (0, h + first))

    def per_head(self, *shape):
        return block((None,) + shape, lambda h, p: (h,) + (0,) * len(shape))

    def whole(self, *shape):
        return block(shape, lambda h, p: (0,) * len(shape))

    def packed(self, rows):
        shift = self.group.bit_length() - 1
        return block(
            (self.group, rows, self.key_size),
            lambda h, p: (h ^ lax.shift_right_logical(p[1], shift), 0, 0),
        )

    def shared(self, rows, width):
        shift = self.group.bit_length() - 1
        spec = block(
            (self.group, rows, width), lambda h, p: (h ^ lax.shift_right_logical(p[1], shift), 0, 0)
        )
        return ((self.count, rows, width), F32, spec)

    def outer(self, place, pieces, packs, gates):
        L, n, width = self.length, self.count, packs[0].shape[1]
        side = pieces[0].shape[1]
        body = functools.partial(outer_kernel, n, TOKEN_ORDER, len(gates))
        tile = block((L, side), lambda t, p: (t, 0))
        specs = [tile] * n + [self.whole(*packs[0].shape)] * n + [self.whole(*g.shape) for g in gates]
        outs = [((n, side, width), F32, self.whole(n, side, width))]
        if gates:
            outs.append(((side, 2 * self.heads), F32, self.whole(side, 2 * self.heads)))
        scratch = [pltpu.VMEM((n, L, width), BF16), pltpu.VMEM((n, HALO, width), F32)]
        flops = 2 * n * L * n * side * width
        return self.call(body, specs, outs, (place, *pieces, *packs, *gates), scratch, flops, (n,))

    def assemble(self, place, parts, widths):
        side, n = parts[0].shape[0], self.count
        body = functools.partial(assemble_kernel, n, widths)
        outs = [((side, n * w), F32, self.whole(side, n * w)) for w in widths]
        scratch = [pltpu.VMEM((n, *parts[0].shape), F32)]
        return self.call(body, [self.whole(*parts[0].shape)] * n, outs, (place, *parts), scratch, 0, (1,))

    def weight_grad(self, place, pieces, packs, widths, gates=()):
        blocks, *gate_grad = self.outer(place, pieces, packs, gates)
        parts = exchange([blocks[k] for k in range(self.count)], "seq")
        return *self.assemble(place, parts, widths), *gate_grad

    def ffn_grads(self, place, ffn_pieces, cot_pieces, w_gate, w_up, w_down):
        L, n, (wide, units) = self.length, self.count, w_gate.shape
        side = wide // n
        tile = block((L, side), lambda t, p: (t, 0))
        once = lambda *shape: pl.BlockSpec(shape, lambda t, p: (0, 0), pipeline_mode=pl.Buffered(1))
        specs = [tile] * (2 * n) + [once(wide, units), once(wide, units), once(units, wide)]
        outs = [
            ((side, units), F32, self.whole(side, units)),
            ((side, units), F32, self.whole(side, units)),
            ((units, side), F32, self.whole(units, side)),
        ]
        scratch = [pltpu.VMEM((L, wide), BF16), pltpu.VMEM((L, wide), BF16)]
        args = (place, *ffn_pieces, *cot_pieces, w_gate, w_up, w_down)
        flops = 6 * n * L * units * (wide + side)
        return self.call(functools.partial(ffn_kernel, n), specs, outs, args, scratch, flops, (n,))

    def front(self):
        key, value, heads = self.key_size, self.value_size, self.heads
        return [
            self.cols(key), self.cols(key), self.cols(value),
            self.rim(key), self.rim(key, heads), self.rim(value, 2 * heads * key // value),
            self.rim(key, 0, self.taps), self.rim(key, 0, self.taps), self.rim(value, 0, self.taps),
            self.whole(self.length, 2 * heads),
        ]

    def call(self, body, in_specs, outs, args, scratch=(), flops=0, grid=None):
        shapes = [jax.ShapeDtypeStruct(shape, dtype) for shape, dtype, _ in outs]
        moved = sum(a.size * a.dtype.itemsize for a in (*args, *shapes))
        return pl.pallas_call(
            body,
            out_shape=shapes,
            grid_spec=pltpu.PrefetchScalarGridSpec(
                num_scalar_prefetch=1,
                grid=grid or (self.heads,),
                in_specs=in_specs,
                out_specs=[spec for _, _, spec in outs],
                scratch_shapes=list(scratch),
            ),
            compiler_params=pltpu.CompilerParams(
                dimension_semantics=("arbitrary",), vmem_limit_bytes=VMEM_LIMIT
            ),
            cost_estimate=pl.CostEstimate(flops=flops, bytes_accessed=moved, transcendentals=0),
        )(*args)

    def local(self, place, *front):
        L, H, K, V = self.length, self.heads, self.key_size, self.value_size
        rows = K + self.rows_per
        body = functools.partial(local_kernel, H, self.group, self.rows_per)
        outs = [
            ((H, L, L), F32, self.per_head(L, L)),
            ((H, L, V), F32, self.per_head(L, V)),
            ((H, L, K), F32, self.per_head(L, K)),
            ((H, L, V), F32, self.per_head(L, V)),
            ((H, L, K), F32, self.per_head(L, K)),
            ((self.count, rows, K), F32, self.packed(rows)),
        ]
        return self.call(body, self.front(), outs, (place, *front), flops=H * L * L * L * 120)

    def scan(self, place, packs, reverse):
        K, R = self.key_size, self.rows_per
        body = functools.partial(scan_kernel, self.count, R, K, reverse)
        spec = self.whole(K + R, K)
        outs = [((self.count, R, K), F32, self.whole(self.count, R, K))]
        scratch = [pltpu.VMEM((self.count, K + R, K), F32)]
        flops = self.count * R * K * K * 6
        return self.call(body, [spec] * self.count, outs, (place, *packs), scratch, flops, (1,))[0]

    def scratch(self):
        return [pltpu.VMEM((self.count, self.rows_per, self.key_size), F32)]

    def part_specs(self):
        return [self.whole(self.rows_per, self.key_size)] * self.count

    def mix(self, place, local_mixed, reach, proj_z, gain, parts):
        L, H, K, V = self.length, self.heads, self.key_size, self.value_size
        body = functools.partial(mix_kernel, self.count, self.group)
        specs = [self.per_head(L, V), self.per_head(L, K), self.cols(V), self.whole(1, V)]
        outs = [
            ((L, H * V), F32, self.cols(V)),
            ((L, H * V), BF16, self.cols(V)),
            ((H, V, K), F32, self.per_head(V, K)),
        ]
        args = (place, local_mixed, reach, proj_z, gain, *parts)
        return self.call(body, specs + self.part_specs(), outs, args, self.scratch(), H * L * K * V * 6)

    def gate_back(self, place, grad_gated, mixed, proj_z, gain, reach):
        L, H, K, V = self.length, self.heads, self.key_size, self.value_size
        body = functools.partial(gate_back_kernel, self.group, self.rows_per)
        specs = [self.cols(V), self.cols(V), self.cols(V), self.whole(1, V), self.per_head(L, K)]
        outs = [
            ((L, H * V), F32, self.cols(V)),
            ((L, H * V), F32, self.cols(V)),
            ((1, V), F32, self.whole(1, V)),
            ((self.count, self.rows_per, K), F32, self.packed(self.rows_per)),
            self.shared(L, V // self.group),
        ]
        args = (place, grad_gated, mixed, proj_z, gain, reach)
        return self.call(body, specs, outs, args, (), H * L * K * V * 6)

    def back(self, place, front, inverse, fresh, erase, grad_mixed, state, parts):
        L, H, K, V, T = self.length, self.heads, self.key_size, self.value_size, self.taps
        body = functools.partial(back_kernel, H, self.group, self.count)
        specs = self.front() + [
            self.per_head(L, L), self.per_head(L, V), self.per_head(L, K), self.cols(V), self.per_head(V, K),
        ]
        outs = [
            ((L, H * K), F32, self.cols(K)),
            ((L, H * K), F32, self.cols(K)),
            ((L, H * V), F32, self.cols(V)),
            ((L, 2 * H), F32, self.whole(L, 2 * H)),
            ((HALO, H * K), F32, self.rim(K)),
            ((HALO, H * K), F32, self.rim(K)),
            ((HALO, H * V), F32, self.rim(V)),
            ((T, H * K), F32, self.rim(K, 0, T)),
            ((T, H * K), F32, self.rim(K, 0, T)),
            ((T, H * V), F32, self.rim(V, 0, T)),
            self.shared(L + HALO, (2 * K + V) // self.group),
        ]
        args = (place, *front, inverse, fresh, erase, grad_mixed, state, *parts)
        flops = H * L * L * L * 100
        return self.call(body, specs + self.part_specs(), outs, args, self.scratch(), flops)


def per_device(
    inputs, norm_in, w_query, w_key, w_value, w_outgate, w_decay, w_write, conv_query, conv_key, conv_value,
    decay_log, decay_bias, norm_out, w_output, norm_ffn, w_gate, w_up, w_down, doc_count, doc_start, cotangent,
):
    length, heads = inputs.shape[0], decay_log.shape[0]
    key_size, value_size = w_query.shape[1] // heads, w_value.shape[1] // heads
    count = lax.axis_size("seq")
    delta = Delta(length, heads, key_size, value_size, conv_query.shape[0], count)
    me = lax.axis_index("seq")
    begin = jnp.where(doc_count[0] > 0, doc_start[0], length)
    place = jnp.stack([begin, me, lax.axis_index("head")]).astype(jnp.int32)
    spreads = count == 8 and lax.axis_size("head") == 4

    resid_in = inputs.astype(F32)
    normed, norm_in_back = jax.vjp(rms_scale, resid_in, norm_in)
    normed_low = normed.astype(BF16)

    def project(weight):
        return jnp.dot(normed_low, weight, preferred_element_type=F32)

    proj_q, proj_k, proj_v = project(w_query), project(w_key), project(w_value)
    w_ab = jnp.concatenate([w_decay, w_write], axis=1)
    proj_ab = project(w_ab)
    proj_z = project(w_outgate)
    tails = [p[length - HALO :] for p in (proj_q, proj_k, proj_v)]
    halo = shifted(jnp.concatenate(tails, axis=1), "seq", 1)
    gates, gates_back = jax.vjp(gate_values, proj_ab, decay_log, decay_bias)
    front = (proj_q, proj_k, proj_v, halo, halo, halo, conv_query, conv_key, conv_value, gates)
    inverse, fresh, erase, local_mixed, reach, pack = delta.local(place, *front)
    packs = exchange([pack[k] for k in range(count)], "seq")
    incoming = delta.scan(place, packs, False)
    parts = exchange([incoming[k] for k in range(count)], "seq")
    gain = norm_out[None]
    mixed, gated_low, state = delta.mix(place, local_mixed, reach, proj_z, gain, parts)

    branch = head_sum(jnp.dot(gated_low, w_output, preferred_element_type=F32))
    middle = resid_in + branch
    normed_ffn, norm_ffn_back = jax.vjp(rms_scale, middle, norm_ffn)
    ffn_low = normed_ffn.astype(BF16)
    grad_hidden = jnp.einsum("td,fd->tf", cotangent, w_down, preferred_element_type=F32)
    gate_pre = jnp.dot(ffn_low, w_gate, preferred_element_type=F32)
    up_pre = jnp.dot(ffn_low, w_up, preferred_element_type=F32)
    hidden, hidden_back = jax.vjp(swiglu, gate_pre, up_pre)
    hidden_low = hidden.astype(BF16)
    grad_gate_pre, grad_up_pre = hidden_back(grad_hidden)
    gate_low, up_low = grad_gate_pre.astype(BF16), grad_up_pre.astype(BF16)
    part_ffn = jnp.einsum("tf,df->td", gate_low, w_gate, preferred_element_type=F32) + jnp.einsum(
        "tf,df->td", up_low, w_up, preferred_element_type=F32
    )
    grad_normed_ffn = head_sum(part_ffn)
    ffn_out = head_sum(jnp.dot(hidden_low, w_down, preferred_element_type=F32))
    block_out = middle + ffn_out
    grad_middle_norm, grad_norm_ffn = norm_ffn_back(grad_normed_ffn)
    grad_middle = cotangent.astype(F32) + grad_middle_norm
    grad_branch = grad_middle.astype(BF16)
    grad_gated = jnp.einsum("td,vd->tv", grad_branch, w_output, preferred_element_type=F32)
    grad_mixed, grad_proj_z, grad_gain, pack_back, share_z = delta.gate_back(place, grad_gated, mixed, proj_z, gain, reach)
    backs = exchange([pack_back[k] for k in range(count)], "seq")
    back_packs = [jnp.concatenate([p[:key_size], b], axis=0) for p, b in zip(packs, backs)]
    outgoing = delta.scan(place, back_packs, True)
    out_parts = exchange([outgoing[k] for k in range(count)], "seq")
    (grad_q, grad_k, grad_v, gates_grad, rim_q, rim_k, rim_v, grad_conv_q, grad_conv_k, grad_conv_v, share_qkv) = delta.back(
        place, front, inverse, fresh, erase, grad_mixed, state, out_parts
    )
    rim = shifted(jnp.concatenate([rim_q, rim_k, rim_v], axis=1), "seq", -1)
    grad_ab, grad_decay_log, grad_decay_bias = gates_back(gates_grad)
    query_cols = proj_q.shape[1]
    pad = ((length - HALO, 0), (0, 0))
    low_q = (grad_q + jnp.pad(rim[:, :query_cols], pad)).astype(BF16)
    low_k = (grad_k + jnp.pad(rim[:, query_cols : 2 * query_cols], pad)).astype(BF16)
    low_v = (grad_v + jnp.pad(rim[:, 2 * query_cols :], pad)).astype(BF16)
    low_z = grad_proj_z.astype(BF16)
    low_ab = grad_ab.astype(BF16)

    def weight_grad(left, right):
        return jnp.einsum("td,tc->dc", left, right, preferred_element_type=F32)

    def input_part(grad_low, weight):
        return jnp.einsum("tc,dc->td", grad_low, weight, preferred_element_type=F32)

    part_in = (
        input_part(low_q, w_query) + input_part(low_k, w_key) + input_part(low_v, w_value)
        + input_part(low_z, w_outgate) + input_part(low_ab, w_ab)
    )
    grad_normed = head_sum(part_in)
    grad_resid, grad_norm_in = norm_in_back(grad_normed)
    grad_inputs = grad_middle + grad_resid

    def scatter(value, dim=0):
        return lax.psum_scatter(value, "seq", scatter_dimension=dim, tiled=True)

    width = inputs.shape[1]
    side = width // count
    taps = jnp.concatenate([grad_conv_q, grad_conv_k, grad_conv_v], axis=1)
    row = jnp.concatenate([grad_gain[0], grad_decay_log, grad_decay_bias])
    row = jnp.pad(row, (0, width - row.shape[0]))
    sums = seq_sum(jnp.concatenate([taps, grad_norm_ffn[None], row[None]], axis=0))
    n_taps, n_gain = taps.shape[0], norm_out.shape[0]
    grad_norm_out = head_total(sums[n_taps + 1 :, :n_gain])[0]
    grad_decay_log = sums[n_taps + 1, n_gain : n_gain + heads]
    grad_decay_bias = sums[n_taps + 1, n_gain + heads : n_gain + 2 * heads]
    key_cols = w_key.shape[1]
    conv_grads = (
        sums[:n_taps, :key_cols], sums[:n_taps, key_cols : 2 * key_cols], sums[:n_taps, 2 * key_cols :],
    )

    def own(vector):
        return lax.dynamic_slice_in_dim(vector, me * side, side, 0)

    grad_norm_ffn = own(sums[n_taps])
    grad_norm_in = own(seq_sum(grad_norm_in.reshape(-1, 128)).reshape(-1))
    grad_w_out = scatter(weight_grad(gated_low, grad_branch), 1)
    if spreads:
        normed_all = spread(normed)
        cot_all = spread(cotangent.astype(F32))
        ffn_all = spread(normed_ffn)
        share_z = exchange([share_z[k] for k in range(count)], "seq")
        grad_w_z = delta.weight_grad(place, normed_all, share_z, (w_outgate.shape[1] // count,))[0]
        share_qkv = exchange([share_qkv[k] for k in range(count)], "seq")
        widths = tuple(w.shape[1] // count for w in (w_query, w_key, w_value))
        all_ab = [grad_ab.T]
        for bit in (4, 2, 1):
            all_ab = all_ab + [swap(jnp.concatenate(all_ab, axis=0), "seq", bit)]
        grad_w_q, grad_w_k, grad_w_v, grad_w_ab = delta.weight_grad(place, normed_all, share_qkv, widths, all_ab)
        grad_w_gate, grad_w_up, grad_w_down = delta.ffn_grads(place, ffn_all, cot_all, w_gate, w_up, w_down)
    else:
        grad_w_ab = scatter(weight_grad(normed_low, low_ab))
        grad_w_q, grad_w_k = scatter(weight_grad(normed_low, low_q)), scatter(weight_grad(normed_low, low_k))
        grad_w_v, grad_w_z = scatter(weight_grad(normed_low, low_v)), scatter(weight_grad(normed_low, low_z))
        grad_w_gate = scatter(weight_grad(ffn_low, gate_low))
        grad_w_up = scatter(weight_grad(ffn_low, up_low))
        grad_w_down = scatter(weight_grad(hidden_low, cotangent), 1)
    return (
        block_out, grad_inputs, grad_norm_in, grad_w_q, grad_w_k, grad_w_v, grad_w_z,
        grad_w_ab[:, :heads], grad_w_ab[:, heads:], *conv_grads, grad_decay_log, grad_decay_bias, grad_norm_out,
        grad_w_out, grad_norm_ffn, grad_w_gate, grad_w_up, grad_w_down,
    )


def solution(mesh):
    rows, cols, split = P("seq", None), P(None, "head"), P("seq", "head")
    return jax.shard_map(
        per_device,
        mesh=mesh,
        in_specs=(
            rows, P(), cols, cols, cols, cols, cols, cols, cols, cols, cols, P("head"), P("head"), P(),
            P("head", None), P(), cols, cols, P("head", None), P("seq"), P("seq"), rows,
        ),
        out_specs=(
            rows, rows, P("seq"), split, split, split, split, split, split, cols, cols, cols, P("head"), P("head"),
            P(), P("head", "seq"), P("seq"), split, split, P("head", "seq"),
        ),
        check_vma=False,
    )
```

```python
import functools
import jax
import jax.numpy as jnp
from jax import lax
from jax.experimental import pallas as pl
from jax.experimental.pallas import tpu as pltpu
from jax.sharding import PartitionSpec as P


F32 = jnp.float32
BF16 = jnp.bfloat16
HALO = 8
VMEM_LIMIT = 56 * 1024 * 1024


def split_low(a):
    high = a.astype(BF16)
    return high, (a - high.astype(F32)).astype(BF16)


def dot_low(a, b, ca, cb):
    return lax.dot_general(
        a.astype(BF16), b.astype(BF16), (((ca,), (cb,)), ((), ())), preferred_element_type=F32
    )


def dot_fine(a, b, ca, cb):
    ah, al = split_low(a)
    bh, bl = split_low(b)
    dims = (((ca,), (cb,)), ((), ()))
    one = functools.partial(lax.dot_general, dimension_numbers=dims, preferred_element_type=F32)
    return one(ah, bh) + (one(ah, bl) + one(al, bh))


def tiles_of(count):
    return count // 2


def grid_iota(size):
    return (
        lax.broadcasted_iota(jnp.int32, (size, size), 0),
        lax.broadcasted_iota(jnp.int32, (size, size), 1),
    )


def lane_pick(x, index):
    lanes = lax.broadcasted_iota(jnp.int32, x.shape, 1)
    return jnp.sum(jnp.where(lanes == index, x, 0.0), axis=1, keepdims=True)


def to_row(column, eye):
    return jnp.sum(jnp.where(eye, column, 0.0), axis=0, keepdims=True)


def agree_mask(length, steps, start):
    at = lax.broadcasted_iota(jnp.int32, (length, 1), 0)
    return ((at >= start) == (at - steps >= start)).astype(F32)


def conv_forward(extended, weight, start):
    length, taps = extended.shape[0] - HALO, weight.shape[0]
    total = None
    for steps in range(taps):
        moved = extended if steps == 0 else pltpu.roll(extended, steps, 0)
        term = moved[HALO:] * weight[taps - 1 - steps : taps - steps] * agree_mask(length, steps, start)
        total = term if total is None else total + term
    return total


def conv_backward(grad, extended, weight, start):
    rows, taps = extended.shape[0], weight.shape[0]
    length = rows - HALO
    total, per_tap = None, [None] * taps
    for steps in range(taps):
        masked = grad * agree_mask(length, steps, start)
        moved = extended if steps == 0 else pltpu.roll(extended, steps, 0)
        per_tap[taps - 1 - steps] = jnp.sum(masked * moved[HALO:], axis=0, keepdims=True)
        term = jnp.concatenate([jnp.zeros((HALO, grad.shape[1]), F32), masked], axis=0)
        term = term * weight[taps - 1 - steps : taps - steps]
        term = term if steps == 0 else pltpu.roll(term, rows - steps, 0)
        total = term if total is None else total + term
    return total, jnp.concatenate(per_tap, axis=0)


def unit_forward(values):
    return values * lax.rsqrt(jnp.sum(values * values, axis=-1, keepdims=True) + 1e-06)


def unit_backward(grad, values):
    scale = lax.rsqrt(jnp.sum(values * values, axis=-1, keepdims=True) + 1e-06)
    unit = values * scale
    return scale * (grad - unit * jnp.sum(unit * grad, axis=-1, keepdims=True))


def silu_slope(pre):
    gate = jax.nn.sigmoid(pre)
    return gate * (1.0 + pre * (1.0 - gate))


def head_terms(step_log, start, length):
    rows, cols = grid_iota(length)
    eye = rows == cols
    running = jnp.sum(jnp.where(rows >= cols, to_row(step_log, eye), 0.0), axis=1, keepdims=True)
    running_row = to_row(running, eye)
    same = (rows >= start) == (cols >= start)
    inclusive = (rows >= cols) & same
    within = jnp.where(inclusive, jnp.exp(jnp.where(inclusive, running - running_row, 0.0)), 0.0)
    below = jnp.where(rows > cols, within, 0.0)
    at = lax.broadcasted_iota(jnp.int32, (length, 1), 0)
    carried = jnp.exp(running) * (at < start).astype(F32)
    total = jnp.sum(step_log, axis=0, keepdims=True)
    last_old = length - 1 < start
    ending = jnp.exp(total - running) * ((at < start) == last_old).astype(F32)
    keeping = jnp.exp(total) * jnp.where(last_old, 1.0, 0.0)
    return within, below, carried, ending, keeping


def tri_inverse(lower, length):
    rows, cols = grid_iota(length)
    near = (rows >> 1) == (cols >> 1)
    start = jnp.where(rows == cols, 1.0, 0.0) - jnp.where(near, lower, 0.0)

    def merge(level, inverse):
        apart = lax.shift_right_logical(rows, level) != lax.shift_right_logical(cols, level)
        joined = lax.shift_right_logical(rows, level + 1) == lax.shift_right_logical(cols, level + 1)
        off = jnp.where(apart & joined, lower, 0.0)
        return inverse - dot_fine(inverse, dot_fine(off, inverse, 1, 0), 1, 0)

    return lax.fori_loop(1, length.bit_length() - 1, merge, start)


def prepared(q_ref, k_ref, v_ref, hq_ref, hk_ref, hv_ref, cq_ref, ck_ref, cv_ref, start):
    ext_q = jnp.concatenate([hq_ref[...], q_ref[...]], axis=0)
    ext_k = jnp.concatenate([hk_ref[...], k_ref[...]], axis=0)
    ext_v = jnp.concatenate([hv_ref[...], v_ref[...]], axis=0)
    pre_q = conv_forward(ext_q, cq_ref[...], start)
    pre_k = conv_forward(ext_k, ck_ref[...], start)
    pre_v = conv_forward(ext_v, cv_ref[...], start)
    return (ext_q, ext_k, ext_v), (pre_q, pre_k, pre_v)


def local_kernel(
    heads, group, rows_per,
    place_ref, q_ref, k_ref, v_ref, hq_ref, hk_ref, hv_ref, cq_ref, ck_ref, cv_ref, gates_ref,
    inverse_ref, fresh_ref, erase_ref, mixed_ref, reach_ref, pack_ref,
):
    head = pl.program_id(0)
    start = place_ref[0]
    length, key_size = q_ref.shape
    _, (pre_q, pre_k, pre_v) = prepared(
        q_ref, k_ref, v_ref, hq_ref, hk_ref, hv_ref, cq_ref, ck_ref, cv_ref, start
    )
    queries = unit_forward(jax.nn.silu(pre_q)) * key_size ** (-0.5)
    keys = unit_forward(jax.nn.silu(pre_k))
    values = jax.nn.silu(pre_v)
    step_log = lane_pick(gates_ref[...], head)
    rate = lane_pick(gates_ref[...], head + heads)
    within, below, carried, ending, keeping = head_terms(step_log, start, length)
    inverse = tri_inverse(rate * below * dot_fine(keys, keys, 1, 1), length)
    fresh = dot_fine(inverse, rate * values, 1, 0)
    erase = dot_fine(inverse, rate * carried * keys, 1, 0)
    attend = within * dot_fine(queries, keys, 1, 1)
    inverse_ref[...] = inverse
    fresh_ref[...] = fresh
    erase_ref[...] = erase
    mixed_ref[...] = dot_fine(attend, fresh, 1, 0)
    reach_ref[...] = carried * queries - dot_fine(attend, erase, 1, 0)
    ended = ending * keys
    r, c = grid_iota(key_size)
    moved = jnp.where(r == c, keeping, 0.0) - dot_fine(erase, ended, 0, 0)
    added = dot_fine(fresh, ended, 0, 0)
    for g in range(group):
        pack_ref[g, :key_size] = moved
        pack_ref[g, key_size:] = added[g * rows_per : (g + 1) * rows_per]


def scan_kernel(reverse, skip, place_ref, move_ref, rows_ref, out_ref):
    count, rows_per, key_size = out_ref.shape

    def lap(i, state):
        shard = count - 1 - i if reverse else i
        out_ref[shard] = state
        return dot_fine(state, move_ref[shard, :key_size], 1, 1 if reverse else 0) + rows_ref[shard, skip:]

    lax.fori_loop(0, count, lap, jnp.zeros((rows_per, key_size), F32))


def mix_kernel(place_ref, mixed_ref, reach_ref, z_ref, gain_ref, state_ref, out_ref, gated_ref, gated_wide_ref):
    mixed = mixed_ref[...] + dot_fine(reach_ref[...], state_ref[...], 1, 1)
    out_ref[...] = mixed
    scaled = mixed * lax.rsqrt(jnp.mean(mixed * mixed, axis=-1, keepdims=True) + 1e-05) * gain_ref[...]
    gated = (scaled * jax.nn.silu(z_ref[...])).astype(gated_ref.dtype)
    gated_ref[...] = gated
    gated_wide_ref[...] = gated.astype(F32)


def gate_back_kernel(
    group, rows_per, place_ref, grad_ref, mixed_ref, z_ref, gain_ref, reach_ref,
    grad_mixed_ref, grad_z_ref, grad_gain_ref, pack_ref, share_ref,
):
    head = pl.program_id(0)
    mixed, z, grad, gain = mixed_ref[...], z_ref[...], grad_ref[...], gain_ref[...]
    scale = lax.rsqrt(jnp.mean(mixed * mixed, axis=-1, keepdims=True) + 1e-05)
    unit = mixed * scale
    gate = jax.nn.silu(z)
    part = jnp.sum(grad * gate * unit, axis=0, keepdims=True)

    @pl.when(head == 0)
    def _():
        grad_gain_ref[...] = part

    @pl.when(head > 0)
    def _():
        grad_gain_ref[...] += part

    grad_z = grad * gain * unit * silu_slope(z)
    grad_z_ref[...] = grad_z
    width = share_ref.shape[2]
    for g in range(group):
        share_ref[g] = grad_z[:, g * width : (g + 1) * width]
    inner = grad * gate * gain
    grad_mixed = scale * (inner - unit * jnp.mean(inner * unit, axis=-1, keepdims=True))
    grad_mixed_ref[...] = grad_mixed
    back = dot_fine(grad_mixed, reach_ref[...], 0, 0)
    for g in range(group):
        pack_ref[g] = back[g * rows_per : (g + 1) * rows_per]


def back_kernel(
    heads, group,
    place_ref, q_ref, k_ref, v_ref, hq_ref, hk_ref, hv_ref, cq_ref, ck_ref, cv_ref, gates_ref,
    inverse_ref, fresh_ref, erase_ref, grad_ref, state_ref, leaving_ref,
    gq_ref, gk_ref, gv_ref, gates_grad_ref, rim_q_ref, rim_k_ref, rim_v_ref,
    gcq_ref, gck_ref, gcv_ref, share_ref,
):
    head = pl.program_id(0)
    start = place_ref[0]
    length, key_size = q_ref.shape
    exts, (pre_q, pre_k, pre_v) = prepared(
        q_ref, k_ref, v_ref, hq_ref, hk_ref, hv_ref, cq_ref, ck_ref, cv_ref, start
    )
    act_q, act_k, values = jax.nn.silu(pre_q), jax.nn.silu(pre_k), jax.nn.silu(pre_v)
    key_scale = key_size ** (-0.5)
    queries = unit_forward(act_q) * key_scale
    keys = unit_forward(act_k)
    step_log = lane_pick(gates_ref[...], head)
    rate = lane_pick(gates_ref[...], head + heads)
    within, below, carried, ending, keeping = head_terms(step_log, start, length)
    key_key = dot_fine(keys, keys, 1, 1)
    query_key = dot_fine(queries, keys, 1, 1)
    state, grad_mixed, inverse = state_ref[...], grad_ref[...], inverse_ref[...]
    leaving = leaving_ref[...]
    key_state = dot_fine(keys, state, 1, 1)
    query_state = dot_fine(queries, state, 1, 1)
    updates = fresh_ref[...] - dot_fine(erase_ref[...], state, 1, 1)
    attend = within * query_key
    end_pull = dot_fine(keys, leaving, 1, 1)
    grad_updates = dot_fine(attend, grad_mixed, 0, 0) + ending * end_pull
    grad_targets = dot_fine(inverse, grad_updates, 0, 0)
    grad_attend = dot_fine(grad_mixed, updates, 1, 1)
    grad_system = -dot_fine(grad_targets, updates, 1, 1)
    held_values = values - carried * key_state
    grad_queries = carried * dot_fine(grad_mixed, state, 1, 0)
    grad_rate = jnp.sum(grad_targets * held_values, axis=1, keepdims=True)
    grad_values = rate * grad_targets
    pull = -(carried * grad_values)
    grad_keys = dot_fine(pull, state, 1, 0) + ending * dot_fine(updates, leaving, 1, 0)
    grad_carried = jnp.sum(grad_mixed * query_state - grad_values * key_state, axis=1, keepdims=True)
    grad_ending = jnp.sum(updates * end_pull, axis=1, keepdims=True)
    grad_keeping = jnp.sum(jnp.sum(state * leaving, axis=1, keepdims=True), axis=0, keepdims=True)
    base = grad_system * below
    grad_rate = grad_rate + jnp.sum(base * key_key, axis=1, keepdims=True)
    base = rate * base
    grad_keys = grad_keys + dot_fine(base, keys, 1, 0) + dot_fine(base, keys, 0, 0)
    pairs = grad_attend * within
    grad_queries = grad_queries + dot_fine(pairs, keys, 1, 0)
    grad_keys = grad_keys + dot_fine(pairs, queries, 0, 0)
    rows, cols = grid_iota(length)
    eye = rows == cols
    powers = jnp.where(rows > cols, base * key_key + pairs * query_key, 0.0)
    column_sum = jnp.sum(powers, axis=0, keepdims=True)
    from_columns = jnp.sum(jnp.where(eye, column_sum, 0.0), axis=1, keepdims=True)
    end_part = grad_ending * ending
    grad_running = jnp.sum(powers, axis=1, keepdims=True) - from_columns + grad_carried * carried - end_part
    whole = jnp.sum(end_part, axis=0, keepdims=True) + grad_keeping * keeping
    running_row = to_row(grad_running, eye)
    grad_step = jnp.sum(jnp.where(cols >= rows, running_row, 0.0), axis=1, keepdims=True) + whole

    lanes = lax.broadcasted_iota(jnp.int32, gates_grad_ref.shape, 1)
    mine = jnp.where(lanes == head, grad_step, 0.0) + jnp.where(lanes == head + heads, grad_rate, 0.0)

    @pl.when(head == 0)
    def _():
        gates_grad_ref[...] = mine

    @pl.when(head > 0)
    def _():
        gates_grad_ref[...] += mine

    grad_pre_q = unit_backward(grad_queries * key_scale, act_q) * silu_slope(pre_q)
    grad_pre_k = unit_backward(grad_keys, act_k) * silu_slope(pre_k)
    grad_pre_v = grad_values * silu_slope(pre_v)
    first = 0
    for grad_pre, ext, weight_ref, out_ref, rim_ref, tap_ref in (
        (grad_pre_q, exts[0], cq_ref, gq_ref, rim_q_ref, gcq_ref),
        (grad_pre_k, exts[1], ck_ref, gk_ref, rim_k_ref, gck_ref),
        (grad_pre_v, exts[2], cv_ref, gv_ref, rim_v_ref, gcv_ref),
    ):
        moved, taps = conv_backward(grad_pre, ext, weight_ref[...], start)
        out_ref[...] = moved[HALO:]
        rim_ref[...] = moved[:HALO]
        tap_ref[...] = taps
        width = grad_pre.shape[1] // group
        for g in range(group):
            piece = moved[:, g * width : (g + 1) * width]
            share_ref[g, :length, first : first + width] = piece[HALO:]
            share_ref[g, length:, first : first + width] = piece[:HALO]
        first += width


def outer_kernel(gates, place_ref, *refs):
    owns, others, share_ref, out_ref = refs[:8], refs[8:16], refs[16], refs[17]
    (gate_out_ref, held, held_gates, total) = refs[18:] if gates else (None, refs[18], None, refs[19])
    seams = gates > 0
    tile, me, rank = pl.program_id(0), place_ref[1], place_ref[2]
    tiles, (count, side, _) = pl.num_programs(0), out_ref.shape
    per_tile = owns[0].shape[0]
    length = per_tile * tiles_of(count) // count

    @pl.when(tile == 0)
    def _():
        for n in range(count):
            shard = 2 * (n % (count // 2)) + ((me & 1) ^ (n // (count // 2)))
            value = share_ref[shard, :length]
            if seams:
                rim = share_ref[jnp.minimum(shard + 1, count - 1), length : length + HALO]
                rim = jnp.where(shard + 1 < count, rim, 0.0)
                value = jnp.concatenate([value[: length - HALO], value[length - HALO :] + rim], axis=0)
            at = n * length
            span = slice(at % per_tile, at % per_tile + length)
            held[at // per_tile, :, span] = value.T.astype(BF16)
            if gates:
                held_gates[at // per_tile, :, span] = share_ref[shard, length + HALO :]
        total[...] = jnp.zeros_like(total)
        if gates:
            gate_out_ref[...] = jnp.zeros_like(gate_out_ref)

    share = held[tile]
    near = tile < tiles_of(count) // 2
    for r in range(4):
        for half in range(2):
            slot = ((rank ^ r) << 1) | half
            n = 2 * r + half
            piece = jnp.where(near, owns[n][...], others[n][...]).astype(BF16)
            total[slot] += dot_low(share, piece, 1, 0)
            if gates:

                @pl.when(slot == me)
                def _(piece=piece):
                    gate_out_ref[...] += dot_low(held_gates[tile], piece, 1, 0)

    @pl.when(tile == tiles - 1)
    def _():
        for t in range(count):
            out_ref[t] = total[t].T


def out_kernel(group, place_ref, *refs):
    near_ref, far_ref = refs[:2]
    firsts, seconds = refs[2 : 2 + group], refs[2 + group : 2 + 2 * group]
    own_ref, other_ref = refs[2 + 2 * group :]
    same = ((place_ref[1] ^ place_ref[2]) & 1) == 0
    length = firsts[0].shape[0]
    own = other = None
    for n in range(group):
        side = near_ref if n < group // 2 else far_ref
        left = side[(n % (group // 2)) * length : (n % (group // 2) + 1) * length].astype(BF16)
        first, second = firsts[n][...], seconds[n][...]
        mine = dot_low(left, jnp.where(same, first, second), 0, 0)
        theirs = dot_low(left, jnp.where(same, second, first), 0, 0)
        own = mine if own is None else own + mine
        other = theirs if other is None else other + theirs
    own_ref[...] = own
    other_ref[...] = other


def assemble_kernel(widths, place_ref, parts_ref, *out_refs):
    for d in range(parts_ref.shape[0]):
        first = 0
        for out_ref, width in zip(out_refs, widths):
            out_ref[:, d * width : (d + 1) * width] = parts_ref[d, :, first : first + width]
            first += width


def ffn_kernel(last, side, place_ref, *refs):
    ffn_refs, cot_refs, (gate_w, up_w, down_w) = refs[:8], refs[8:16], refs[16:19]
    if last:
        before, grad_gate_ref, grad_up_ref, grad_down_ref, ffn, cot, sums = refs[19:]
    else:
        sums, ffn, cot = refs[19:]
    me, rank = place_ref[1], place_ref[2]
    for r in range(4):
        for half in range(2):
            at = pl.ds(pl.multiple_of((((rank ^ r) << 1) | half) * side, side), side)
            ffn[:, at] = ffn_refs[2 * r + half][...].astype(BF16)
            cot[:, at] = cot_refs[2 * r + half][...].astype(BF16)
    gate_pre = dot_low(ffn[...], gate_w[...], 1, 1)
    up_pre = dot_low(ffn[...], up_w[...], 1, 1)
    grad_hidden = dot_low(cot[...], down_w[...], 1, 1)
    gate = jax.nn.sigmoid(gate_pre)
    active = gate_pre * gate
    hidden = (active * up_pre).astype(BF16)
    grad_up = (grad_hidden * active).astype(BF16)
    slope = gate * (1.0 + gate_pre * (1.0 - gate))
    grad_gate = (grad_hidden * up_pre * slope).astype(BF16)
    mine = pl.ds(pl.multiple_of(me * side, side), side)
    ffn_mine, cot_mine = ffn[:, mine], cot[:, mine]

    @pl.when(pl.program_id(0) == 0)
    def _():
        sums[...] = before[...] if last else jnp.zeros_like(sums)

    sums[0] += dot_low(ffn_mine, grad_gate, 0, 0)
    sums[1] += dot_low(ffn_mine, grad_up, 0, 0)
    sums[2] += dot_low(cot_mine, hidden, 0, 0)

    if last:

        @pl.when(pl.program_id(0) == pl.num_programs(0) - 1)
        def _():
            grad_gate_ref[...] = sums[0].T
            grad_up_ref[...] = sums[1].T
            grad_down_ref[...] = sums[2].T


def swap(value, axis, bit):
    size = lax.axis_size(axis)
    return lax.ppermute(value, axis, [(at, at ^ bit) for at in range(size)])


def shifted(value, axis, steps):
    count = lax.axis_size(axis)
    first, last = (max(0, -steps), min(count, count - steps))
    return lax.ppermute(value, axis, [(source, source + steps) for source in range(first, last)])


def exchange(parts):
    return lax.all_to_all(parts, "seq", 0, 0, tiled=True)


def head_sum(part):
    count, half = lax.axis_size("head"), part.shape[0] // 2
    mine = lax.axis_index("head") & 1
    kept = lax.dynamic_slice_in_dim(part, mine * half, half, 0)
    kept = kept + swap(lax.dynamic_slice_in_dim(part, (1 - mine) * half, half, 0), "head", 1)
    bit = 2
    while bit < count:
        kept = kept + swap(kept, "head", bit)
        bit *= 2
    other = swap(kept, "head", 1)
    low = mine == 0
    return jnp.concatenate([jnp.where(low, kept, other), jnp.where(low, other, kept)], axis=0)


def all_sum(value, axis):
    bit = 1
    while bit < lax.axis_size(axis):
        value = value + swap(value, axis, bit)
        bit *= 2
    return value


FFN_TILE = 256


def stacked(value, bit):
    other = swap(value, "seq", bit)
    return jnp.concatenate([value, other], axis=0)


def quarter(value):
    width = value.shape[1] // 4
    return lax.dynamic_slice_in_dim(value, lax.axis_index("head") * width, width, 1)


def spread(mine, plan):
    count, width = lax.axis_size("seq"), mine.shape[1]
    lines = [list(range(y, count, 2)) for y in range(2)]
    line = lax.all_gather(mine, "seq", axis=0, tiled=True, axis_index_groups=lines)
    rows = line.shape[0]

    def crossed(value):
        return swap(value, "head", 1)

    def both(first, second):
        return jnp.concatenate([first, second], axis=0)

    def x_then_y(part):
        own = both(part, swap(part, "head", 2))
        other = swap(own, "seq", 1)
        own_c, other_c = crossed(own), crossed(other)
        return [(own, 0, other, 0), (own_c, 0, other_c, 0), (own, rows, other, rows), (own_c, rows, other_c, rows)]

    if plan == "xy":
        have = x_then_y(line)
        return [(*have[r], half) for r in range(4) for half in range(2)]
    part = line[:, : width // 2]
    whole = both(part, swap(part, "seq", 1))
    other = swap(whole, "head", 2)
    first = [(p, 0, p, rows) for p in (whole, crossed(whole), other, crossed(other))]
    second = x_then_y(line[:, width // 2 :])
    return [(*(first, second)[half][r], 0) for r in range(4) for half in range(2)]


def rms_scale(values, gain):
    return values * lax.rsqrt(jnp.mean(values * values, axis=-1, keepdims=True) + 1e-05) * gain


def swiglu(gate_pre, up_pre):
    return jax.nn.silu(gate_pre) * up_pre


def gate_values(proj_ab, decay_log, decay_bias):
    heads = decay_log.shape[0]
    decays = -jnp.exp(decay_log) * jax.nn.softplus(proj_ab[:, :heads] + decay_bias)
    return jnp.concatenate([decays, jax.nn.sigmoid(proj_ab[:, heads:])], axis=1)


def block(shape, index):
    return pl.BlockSpec(shape, index)


class Delta:
    def __init__(self, length, heads, key_size, value_size, taps, count):
        self.length, self.heads, self.count = length, heads, count
        self.key_size, self.value_size, self.taps = key_size, value_size, taps
        self.group = count // heads
        self.rows_per = heads * value_size // count
        assert self.group * heads == count and self.group & (self.group - 1) == 0

    def cols(self, width, first=0):
        return block((self.length, width), lambda h, p: (0, h + first))

    def rim(self, width, first=0, rows=HALO):
        return block((rows, width), lambda h, p: (0, h + first))

    def per_head(self, *shape):
        return block((None,) + shape, lambda h, p: (h,) + (0,) * len(shape))

    def whole(self, *shape):
        return block(shape, lambda h, p: (0,) * len(shape))

    def packed(self, rows):
        return block((self.group, rows, self.key_size), lambda h, p: (h, 0, 0))

    def shared(self, rows, width):
        spec = block((self.group, rows, width), lambda h, p: (h, 0, 0))
        return ((self.count, rows, width), F32, spec)

    def outer(self, place, pieces, share, gates):
        L, n, width = self.length, self.count, share.shape[2]
        tiles = tiles_of(n)
        rows, side = n * L // tiles, pieces[0][0].shape[1] // (1 + pieces[1][4])
        body = functools.partial(outer_kernel, gates)
        near = [
            block((rows, side), functools.partial(lambda f, c, t, p: (f + jnp.minimum(t, 1), c), own // rows, col))
            for _, own, _, _, col in pieces
        ]
        far = [
            block((rows, side), functools.partial(lambda f, c, t, p: (f + jnp.maximum(t - 2, 0), c), other // rows, col))
            for _, _, _, other, col in pieces
        ]
        specs = near + far + [self.whole(*share.shape)]
        outs = [((n, side, width), F32, self.whole(n, side, width))]
        if gates:
            outs.append(((gates, side), F32, self.whole(gates, side)))
        scratch = [
            pltpu.VMEM((tiles, width, rows), BF16),
            *([pltpu.VMEM((tiles, gates, rows), F32)] if gates else []),
            pltpu.VMEM((n, width, side), F32),
        ]
        flops = 2 * n * L * n * side * width
        args = (place, *[p[0] for p in pieces], *[p[2] for p in pieces], share)
        return self.call(body, specs, outs, args, scratch, flops, (tiles,))

    def assemble(self, place, parts, widths):
        n, side, _ = parts.shape
        outs = [((side, n * w), F32, self.whole(side, n * w)) for w in widths]
        body = functools.partial(assemble_kernel, widths)
        return self.call(body, [self.whole(*parts.shape)], outs, (place, parts), (), 0, (1,))

    def weight_grad(self, place, pieces, share, widths, gates=0):
        blocks, *gate_grad = self.outer(place, pieces, share, gates)
        parts = exchange(blocks)
        return *self.assemble(place, parts, widths), *gate_grad

    def out_grads(self, place, near, far, firsts, seconds):
        cols, group, side = near.shape[1], len(firsts), firsts[0].shape[1]
        step = min(256, cols)
        tall = block((near.shape[0], step), lambda v, p: (0, v))
        result = block((step, side), lambda v, p: (v, 0))
        specs = [tall, tall] + [self.whole(self.length, side)] * (2 * group)
        outs = [((cols, side), F32, result), ((cols, side), F32, result)]
        args = (place, near, far, *firsts, *seconds)
        flops = 4 * group * self.length * cols * side
        return self.call(functools.partial(out_kernel, group), specs, outs, args, (), flops, (cols // step,))

    def ffn_grads(self, place, ffn_all, cot_all, w_gate, w_up, w_down, before=None):
        L, n, (wide, units) = self.length, self.count, w_gate.shape
        side, last = wide // n, before is not None
        steps = n * L // 2 // FFN_TILE
        at = 2 if last else 0
        specs = [
            block((FFN_TILE, side), functools.partial(lambda f, c, t, p: (f + t, c), piece[at + 1] // FFN_TILE, piece[4]))
            for piece in (*ffn_all, *cot_all)
        ]
        once = pl.BlockSpec((units, wide), lambda t, p: (0, 0), pipeline_mode=pl.Buffered(1))
        specs = specs + [once, once, once]
        scratch = [pltpu.VMEM((FFN_TILE, wide), BF16), pltpu.VMEM((FFN_TILE, wide), BF16)]
        sums = (3, side, units)
        args = (place, *[p[at] for p in (*ffn_all, *cot_all)], w_gate.T, w_up.T, w_down)
        if last:
            args = (*args, before)
            specs = specs + [pl.BlockSpec(sums, lambda t, p: (0, 0, 0), pipeline_mode=pl.Buffered(1))]
            outs = [((units, side), F32, pl.BlockSpec((units, side), lambda t, p: (0, 0)))] * 3
            scratch = scratch + [pltpu.VMEM(sums, F32)]
        else:
            outs = [(sums, F32, self.whole(*sums))]
        flops = 3 * n * L * units * (wide + side)
        body = functools.partial(ffn_kernel, last, side)
        return self.call(body, specs, outs, args, scratch, flops, (steps,))

    def front(self):
        key, value, heads = self.key_size, self.value_size, self.heads
        return [
            self.cols(key), self.cols(key), self.cols(value),
            self.rim(key), self.rim(key, heads), self.rim(value, 2 * heads * key // value),
            self.rim(key, 0, self.taps), self.rim(key, 0, self.taps), self.rim(value, 0, self.taps),
            self.whole(self.length, 2 * heads),
        ]

    def call(self, body, in_specs, outs, args, scratch=(), flops=0, grid=None):
        shapes = [jax.ShapeDtypeStruct(shape, dtype) for shape, dtype, _ in outs]
        moved = sum(a.size * a.dtype.itemsize for a in (*args, *shapes))
        return pl.pallas_call(
            body,
            out_shape=shapes,
            grid_spec=pltpu.PrefetchScalarGridSpec(
                num_scalar_prefetch=1,
                grid=grid or (self.heads,),
                in_specs=in_specs,
                out_specs=[spec for _, _, spec in outs],
                scratch_shapes=list(scratch),
            ),
            compiler_params=pltpu.CompilerParams(
                dimension_semantics=("arbitrary",), vmem_limit_bytes=VMEM_LIMIT
            ),
            cost_estimate=pl.CostEstimate(flops=flops, bytes_accessed=moved, transcendentals=0),
        )(*args)

    def local(self, place, *front):
        L, H, K, V = self.length, self.heads, self.key_size, self.value_size
        rows = K + self.rows_per
        body = functools.partial(local_kernel, H, self.group, self.rows_per)
        outs = [
            ((H, L, L), F32, self.per_head(L, L)),
            ((H, L, V), F32, self.per_head(L, V)),
            ((H, L, K), F32, self.per_head(L, K)),
            ((H, L, V), F32, self.per_head(L, V)),
            ((H, L, K), F32, self.per_head(L, K)),
            ((self.count, rows, K), F32, self.packed(rows)),
        ]
        return self.call(body, self.front(), outs, (place, *front), flops=H * L * L * L * 120)

    def scan(self, place, moves, rows, skip, reverse):
        K, R = self.key_size, self.rows_per
        body = functools.partial(scan_kernel, reverse, skip)
        outs = [((self.count, R, K), F32, self.whole(self.count, R, K))]
        flops = self.count * R * K * K * 6
        specs = [self.whole(*moves.shape), self.whole(*rows.shape)]
        return self.call(body, specs, outs, (place, moves, rows), (), flops, (1,))[0]

    def mix(self, place, local_mixed, reach, proj_z, gain, state):
        L, H, K, V = self.length, self.heads, self.key_size, self.value_size
        specs = [
            self.per_head(L, V), self.per_head(L, K), self.cols(V), self.whole(1, V), self.per_head(V, K),
        ]
        outs = [
            ((L, H * V), F32, self.cols(V)),
            ((L, H * V), BF16, self.cols(V)),
            ((L, H * V), F32, self.cols(V)),
        ]
        args = (place, local_mixed, reach, proj_z, gain, state)
        return self.call(mix_kernel, specs, outs, args, (), H * L * K * V * 6)

    def gate_back(self, place, grad_gated, mixed, proj_z, gain, reach):
        L, H, K, V = self.length, self.heads, self.key_size, self.value_size
        body = functools.partial(gate_back_kernel, self.group, self.rows_per)
        specs = [self.cols(V), self.cols(V), self.cols(V), self.whole(1, V), self.per_head(L, K)]
        outs = [
            ((L, H * V), F32, self.cols(V)),
            ((L, H * V), F32, self.cols(V)),
            ((1, V), F32, self.whole(1, V)),
            ((self.count, self.rows_per, K), F32, self.packed(self.rows_per)),
            self.shared(L, V // self.group),
        ]
        args = (place, grad_gated, mixed, proj_z, gain, reach)
        return self.call(body, specs, outs, args, (), H * L * K * V * 6)

    def back(self, place, front, inverse, fresh, erase, grad_mixed, state, leaving):
        L, H, K, V, T = self.length, self.heads, self.key_size, self.value_size, self.taps
        body = functools.partial(back_kernel, H, self.group)
        specs = self.front() + [
            self.per_head(L, L), self.per_head(L, V), self.per_head(L, K), self.cols(V), self.per_head(V, K),
            self.per_head(V, K),
        ]
        outs = [
            ((L, H * K), F32, self.cols(K)),
            ((L, H * K), F32, self.cols(K)),
            ((L, H * V), F32, self.cols(V)),
            ((L, 2 * H), F32, self.whole(L, 2 * H)),
            ((HALO, H * K), F32, self.rim(K)),
            ((HALO, H * K), F32, self.rim(K)),
            ((HALO, H * V), F32, self.rim(V)),
            ((T, H * K), F32, self.rim(K, 0, T)),
            ((T, H * K), F32, self.rim(K, 0, T)),
            ((T, H * V), F32, self.rim(V, 0, T)),
            self.shared(L + HALO, (2 * K + V) // self.group),
        ]
        args = (place, *front, inverse, fresh, erase, grad_mixed, state, leaving)
        flops = H * L * L * L * 100
        return self.call(body, specs, outs, args, (), flops)


def per_device(
    inputs, norm_in, w_query, w_key, w_value, w_outgate, w_decay, w_write, conv_query, conv_key, conv_value,
    decay_log, decay_bias, norm_out, w_output, norm_ffn, w_gate, w_up, w_down, doc_count, doc_start, cotangent,
):
    length, heads = inputs.shape[0], decay_log.shape[0]
    key_size, value_size = w_query.shape[1] // heads, w_value.shape[1] // heads
    count = lax.axis_size("seq")
    delta = Delta(length, heads, key_size, value_size, conv_query.shape[0], count)
    me = lax.axis_index("seq")
    begin = jnp.where(doc_count[0] > 0, doc_start[0], length)
    place = jnp.stack([begin, me, lax.axis_index("head")]).astype(jnp.int32)
    spreads = count == 8 and lax.axis_size("head") == 4

    return block_grads(
        delta, place, spreads, inputs, norm_in, w_query, w_key, w_value, w_outgate, w_decay, w_write,
        conv_query, conv_key, conv_value, decay_log, decay_bias, norm_out, w_output, norm_ffn, w_gate, w_up,
        w_down, cotangent,
    )


def block_grads(
    delta, place, spreads, inputs, norm_in, w_query, w_key, w_value, w_outgate, w_decay, w_write,
    conv_query, conv_key, conv_value, decay_log, decay_bias, norm_out, w_output, norm_ffn, w_gate, w_up,
    w_down, cotangent,
):
    length, heads, key_size, count = delta.length, delta.heads, delta.key_size, delta.count
    me, wide = lax.axis_index("seq"), inputs.shape[1]
    if spreads:
        cot_all = spread(quarter(cotangent).astype(F32), "xy")
    resid_in = inputs.astype(F32)
    normed, norm_in_back = jax.vjp(rms_scale, resid_in, norm_in)
    normed_low = normed.astype(BF16)
    if spreads:
        nrm_mine, normed_low = lax.optimization_barrier((quarter(normed), normed_low))

    def project(weight):
        return jnp.dot(normed_low, weight, preferred_element_type=F32)

    proj_q, proj_k, proj_v = project(w_query), project(w_key), project(w_value)
    w_ab = jnp.concatenate([w_decay, w_write], axis=1)
    proj_ab = project(w_ab)
    proj_z = project(w_outgate)
    tails = [p[length - HALO :] for p in (proj_q, proj_k, proj_v)]
    halo = shifted(jnp.concatenate(tails, axis=1), "seq", 1)
    gates, gates_back = jax.vjp(gate_values, proj_ab, decay_log, decay_bias)
    front = (proj_q, proj_k, proj_v, halo, halo, halo, conv_query, conv_key, conv_value, gates)
    inverse, fresh, erase, local_mixed, reach, pack = delta.local(place, *front)
    packs = exchange(pack)
    incoming = delta.scan(place, packs, packs, key_size, False)
    state_shape = (heads, delta.value_size, key_size)
    state = exchange(incoming).reshape(state_shape)
    gain = norm_out[None]
    if spreads:
        nrm_mine, state = lax.optimization_barrier((nrm_mine, state))
    mixed, gated_low, gated_wide = delta.mix(place, local_mixed, reach, proj_z, gain, state)
    part_out = jnp.dot(gated_low, w_output, preferred_element_type=F32)
    branch = head_sum(part_out)
    middle = resid_in + branch
    normed_ffn, norm_ffn_back = jax.vjp(rms_scale, middle, norm_ffn)
    ffn_low = normed_ffn.astype(BF16)
    if spreads:
        near_gated = stacked(gated_wide, 4)
        far_gated = swap(near_gated, "seq", 2)
        normed_all = spread(nrm_mine, "mix")
        ffn_all = spread(quarter(normed_ffn), "mix")
    grad_hidden = jnp.einsum("td,fd->tf", cotangent, w_down, preferred_element_type=F32)
    gate_pre = jnp.dot(ffn_low, w_gate, preferred_element_type=F32)
    up_pre = jnp.dot(ffn_low, w_up, preferred_element_type=F32)
    hidden, hidden_back = jax.vjp(swiglu, gate_pre, up_pre)
    hidden_low = hidden.astype(BF16)
    grad_gate_pre, grad_up_pre = hidden_back(grad_hidden)
    gate_low, up_low = grad_gate_pre.astype(BF16), grad_up_pre.astype(BF16)
    part_ffn = jnp.einsum("tf,df->td", gate_low, w_gate, preferred_element_type=F32) + jnp.einsum(
        "tf,df->td", up_low, w_up, preferred_element_type=F32
    )
    grad_normed_ffn = head_sum(part_ffn)
    grad_middle_norm, grad_norm_ffn = norm_ffn_back(grad_normed_ffn)
    grad_middle = cotangent.astype(F32) + grad_middle_norm
    grad_branch = grad_middle.astype(BF16)
    grad_gated = jnp.einsum("td,vd->tv", grad_branch, w_output, preferred_element_type=F32)
    grad_mixed, grad_proj_z, grad_gain, pack_back, share_z = delta.gate_back(
        place, grad_gated, mixed, proj_z, gain, reach
    )
    backs = exchange(pack_back)
    outgoing = delta.scan(place, packs, backs, 0, True)
    leaving = exchange(outgoing).reshape(state_shape)
    (grad_q, grad_k, grad_v, gates_grad, rim_q, rim_k, rim_v, grad_conv_q, grad_conv_k, grad_conv_v,
     share_qkv) = delta.back(place, front, inverse, fresh, erase, grad_mixed, state, leaving)
    hidden_low, grad_q = lax.optimization_barrier((hidden_low, grad_q))
    part_down = jnp.dot(hidden_low, w_down, preferred_element_type=F32)
    block_out = middle + head_sum(part_down)
    rim = shifted(jnp.concatenate([rim_q, rim_k, rim_v], axis=1), "seq", -1)
    grad_ab, grad_decay_log, grad_decay_bias = gates_back(gates_grad)
    query_cols = proj_q.shape[1]
    pad = ((length - HALO, 0), (0, 0))
    low_q = (grad_q + jnp.pad(rim[:, :query_cols], pad)).astype(BF16)
    low_k = (grad_k + jnp.pad(rim[:, query_cols : 2 * query_cols], pad)).astype(BF16)
    low_v = (grad_v + jnp.pad(rim[:, 2 * query_cols :], pad)).astype(BF16)
    low_z = grad_proj_z.astype(BF16)
    low_ab = grad_ab.astype(BF16)

    def weight_grad(left, right):
        return jnp.einsum("td,tc->dc", left, right, preferred_element_type=F32)

    def input_part(grad_low, weight):
        return jnp.einsum("tc,dc->td", grad_low, weight, preferred_element_type=F32)

    part_in = (
        input_part(low_q, w_query) + input_part(low_k, w_key) + input_part(low_v, w_value)
        + input_part(low_z, w_outgate) + input_part(low_ab, w_ab)
    )
    extra = jnp.pad(grad_gain, ((0, 15), (0, wide - grad_gain.shape[1])))
    summed = head_sum(jnp.concatenate([part_in, extra], axis=0))
    grad_normed, gain_row = summed[:length], summed[length : length + 1]
    grad_resid, grad_norm_in = norm_in_back(grad_normed)
    grad_inputs = grad_middle + grad_resid

    def scatter(value, dim=0):
        return lax.psum_scatter(value, "seq", scatter_dimension=dim, tiled=True)

    side = wide // count
    taps = jnp.concatenate([grad_conv_q, grad_conv_k, grad_conv_v], axis=1)
    row = jnp.concatenate([grad_decay_log, grad_decay_bias])
    row = jnp.pad(row, (0, wide - row.shape[0]))
    rows = jnp.concatenate([taps, grad_norm_ffn[None], row[None], gain_row, grad_norm_in[None]], axis=0)
    sums = all_sum(rows, "seq")
    n_taps, n_gain = taps.shape[0], norm_out.shape[0]
    grad_norm_out = sums[n_taps + 2, :n_gain]
    grad_decay_log = sums[n_taps + 1, :heads]
    grad_decay_bias = sums[n_taps + 1, heads : 2 * heads]
    key_cols = w_key.shape[1]
    conv_grads = (
        sums[:n_taps, :key_cols], sums[:n_taps, key_cols : 2 * key_cols], sums[:n_taps, 2 * key_cols :],
    )

    def own(vector):
        return lax.dynamic_slice_in_dim(vector, me * side, side, 0)

    grad_norm_ffn, grad_norm_in = own(sums[n_taps]), own(sums[n_taps + 3])
    if spreads:
        key_widths = tuple(w.shape[1] // count for w in (w_query, w_key, w_value))
        share_z = exchange(share_z)
        share_ab = grad_ab.T
        share_ab = jnp.broadcast_to(share_ab, (count,) + share_ab.shape)
        share_qkv = exchange(jnp.concatenate([share_qkv, share_ab], axis=1))
        core = lax.axis_index("head") & 1

        def branch_block(at):
            return lax.dynamic_slice_in_dim(grad_middle, at * side, side, 1)

        pair = (me >> 1) << 1
        firsts = [branch_block(pair | core)]
        firsts += [swap(branch_block(((me ^ k) >> 1 << 1) | core), "seq", k) for k in (4, 2, 6)]
        crossed = swap(jnp.concatenate(firsts[1:], axis=0), "head", 1)
        seconds = [branch_block(pair | (1 - core))] + [crossed[n * length : (n + 1) * length] for n in range(3)]
        own_out, other_out = delta.out_grads(place, near_gated, far_gated, firsts, seconds)
        grad_w_out = own_out + swap(other_out, "seq", 1)
        grad_w_z = delta.weight_grad(place, normed_all, share_z, (w_outgate.shape[1] // count,))[0]
        grad_w_q, grad_w_k, grad_w_v, grad_w_ab = delta.weight_grad(place, normed_all, share_qkv, key_widths, 2 * heads)
        grad_w_ab = grad_w_ab.T
        part = delta.ffn_grads(place, ffn_all, cot_all, w_gate, w_up, w_down)[0]
        grad_w_gate, grad_w_up, grad_w_down = delta.ffn_grads(
            place, ffn_all, cot_all, w_gate, w_up, w_down, part
        )
        grad_w_gate, grad_w_up = grad_w_gate.T, grad_w_up.T
    else:
        grad_w_ab = scatter(weight_grad(normed_low, low_ab))
        grad_w_q, grad_w_k = scatter(weight_grad(normed_low, low_q)), scatter(weight_grad(normed_low, low_k))
        grad_w_v, grad_w_z = scatter(weight_grad(normed_low, low_v)), scatter(weight_grad(normed_low, low_z))
        grad_w_gate = scatter(weight_grad(ffn_low, gate_low))
        grad_w_up = scatter(weight_grad(ffn_low, up_low))
        grad_w_down = scatter(weight_grad(hidden_low, cotangent), 1)
        grad_w_out = scatter(weight_grad(gated_low, grad_branch), 1)
    return (
        block_out, grad_inputs, grad_norm_in, grad_w_q, grad_w_k, grad_w_v, grad_w_z,
        grad_w_ab[:, :heads], grad_w_ab[:, heads:], *conv_grads, grad_decay_log, grad_decay_bias, grad_norm_out,
        grad_w_out, grad_norm_ffn, grad_w_gate, grad_w_up, grad_w_down,
    )


def solution(mesh):
    rows, cols, split = P("seq", None), P(None, "head"), P("seq", "head")
    return jax.shard_map(
        per_device,
        mesh=mesh,
        in_specs=(
            rows, P(), cols, cols, cols, cols, cols, cols, cols, cols, cols, P("head"), P("head"), P(),
            P("head", None), P(), cols, cols, P("head", None), P("seq"), P("seq"), rows,
        ),
        out_specs=(
            rows, rows, P("seq"), split, split, split, split, split, split, cols, cols, cols, P("head"), P("head"),
            P(), P("head", "seq"), P("seq"), split, split, P("head", "seq"),
        ),
        check_vma=False,
    )
```
